256 devices in a mesh: wide: 64 (over y, z, core), narrow: 4 (over x).
Axes of the slice: x: 4, y: 4, z: 8, core: 2. Of those that a mesh axis runs over, the one named last changes fastest.
Arguments:
- features: bfloat16 [768, 524288], P('narrow', 'wide'), may hold values from -6 to 6
- owner_of: int32 [32768, 16, 1], P('wide'), may hold values from 0 to 63; in each aligned block of 8192 rows (0 to 8191, 8192 to 16383, ..., all dimensions but the last counted through in order) at most 192 rows name the same one
- row_of: int32 [32768, 16], P('wide'), may hold values from 0 to 8191
- w_self: bfloat16 [768, 256], P('narrow'), may hold values from -0.15625 to 0.15625
- w_neighbor: bfloat16 [768, 256], P('narrow'), may hold values from -0.15625 to 0.15625
- cotangent: bfloat16 [32768, 256], P(('wide', 'narrow')), may hold values from -0.032958984 to 0.032958984
Outputs:
- hidden: bfloat16 [32768, 256], P(('wide', 'narrow'))
- grad_self: float32 [768, 256], P('narrow')
- grad_neighbor: float32 [768, 256], P('narrow')
The draws below stay inside these ranges and needn't reach their ends.
Inputs may be any that keep to these rules, and one draw needn't show every extreme that they name: `owner_of`: among the 8192 rows read by the targets of one index of wide, no owner is named more than 192 times, and in every draw some owner is named exactly 192 times by some index.
All inputs are finite; a program needn't handle non-finite values.
Results may differ from the reference program's by a relative error of at most 0.0054.
Values may be sent and summed in bfloat16 or wider, within the bound.
A program may use at most 64 MiB of HBM per device.

```python
import math
import jax
import jax.numpy as jnp
import numpy as np
from jax import lax

F = 768
H = 256
NODE_DEV = 8192
TGT_DEV = 512
FANOUT = 15
REQ = 16
CAP = 192
NODES = 524288
TARGETS = 32768
N_WIDE = 64


def plant(result, rng, low, top_value):
    place = [jax.random.randint(jax.random.fold_in(rng, axis), (), 0, length) for axis, length in enumerate(result.shape)]
    widest = result.shape.index(max(result.shape))
    next_to = place[:widest] + [(place[widest] + 1) % result.shape[widest]] + place[widest + 1:]
    return result.at[tuple(place)].set(low).at[tuple(next_to)].set(top_value)


def block_scale(stream_key, extent, pieces, low, largest):
    def one(position, shards_of):
        steps = jax.random.uniform(jax.random.fold_in(jax.random.fold_in(stream_key, 6), position), (shards_of,), jnp.float32, low / len(pieces), largest / len(pieces))
        return jnp.repeat(jnp.exp(steps), extent[position] // shards_of).reshape((-1,) + (1,) * (len(extent) - position - 1))

    gain = one(*pieces[0])
    for cut in pieces[1:]:
        gain = gain * one(*cut)
    return gain


def shared_out(stream_key, own, number, rows, count, top, limit, lean):
    sequence = jax.random.permutation(stream_key, count)
    heavy_load, ordinary = shares(count, rows * top, limit, lean, True), shares(count, rows * top, limit, lean, False)
    places = jnp.arange(count)

    def named(tallies, turn):
        used = int((tallies > 0).sum())
        fixed = max(1, used // 4)
        passed = fixed + (places - fixed + turn * (used - fixed)) % max(1, count - fixed)
        return jnp.zeros((count,), jnp.int32).at[sequence[jnp.where(places < fixed, places, passed)]].set(jnp.asarray(tallies, jnp.int32))

    tallies = jnp.where(number % 4 == 0, named(heavy_load, number // 4), named(ordinary, number - number // 4 - 1))
    mixed = jax.random.permutation(jax.random.fold_in(own, 3), count)
    source_of, sink = mixed[0:count // 2 * 2:2], mixed[1:count // 2 * 2:2]
    slack = jnp.minimum(tallies[source_of] - 1, limit - tallies[sink]) // 2
    slack = jnp.where((source_of == sequence[0]) | (sink == sequence[0]) | (tallies[sink] == 0), 0, jnp.maximum(slack, 0))
    passed = jax.random.randint(jax.random.fold_in(own, 4), (count // 2,), 0, 1 << 20) % (slack + 1)
    tallies = tallies.at[source_of].add(-passed).at[sink].add(passed)
    members = jnp.searchsorted(jnp.cumsum(tallies), jnp.arange(rows * top), side="right").astype(jnp.int32)
    listing = members.reshape(top, rows).T
    listing = listing[jax.random.permutation(jax.random.fold_in(own, 1), rows)]
    turn = jax.random.randint(jax.random.fold_in(own, 2), (rows, 1), 0, top)
    return jnp.take_along_axis(listing, (jnp.arange(top)[None, :] + turn) % top, axis=1)


def shares(number_of, total, limit, skew, full):
    portions = [(1 << 20) // math.isqrt(rank ** skew) + 1 for rank in range(1, number_of + 1)]
    largest = limit if full else min(limit, max(-(-total // number_of), total * portions[0] // sum(portions)))
    least = 1 if total - largest >= number_of - 1 else 0
    counts, rest = [largest] + [least] * (number_of - 1), total - largest - least * (number_of - 1)
    while rest > 0:
        candidates = [i for i in range(1, number_of) if counts[i] < largest] or [i for i in range(1, number_of) if counts[i] < limit]
        mass, remaining = sum([portions[i] for i in candidates]), rest
        for i in candidates:
            extra = min(limit - counts[i], max(1, remaining * portions[i] // mass), rest)
            counts[i] = counts[i] + extra
            rest = rest - extra
    return np.array(counts)


def bell_draw(own_key, dims, scale, limit, shards=(), kind=jnp.bfloat16):
    entries = scale * jax.random.normal(own_key, dims, jnp.float32)
    if shards:
        entries = entries * block_scale(own_key, dims, shards, -0.22, 0.18)
    return jnp.clip(entries, -limit, limit).astype(kind)


def setup_inputs(seed: int = 0) -> dict:
    streams_of = jax.random.split(jax.random.key(seed), 7)
    features = bell_draw(streams_of[0], (F, NODES), 1.0, 6.0, ((0, 4), (1, 64)))
    owner_of_keys = jax.random.split(jax.random.fold_in(streams_of[1], 1), TARGETS * REQ // (TGT_DEV * REQ))
    owner_of_turns = jax.random.permutation(jax.random.fold_in(streams_of[1], 3), TARGETS * REQ // (TGT_DEV * REQ))
    owner_of = jax.vmap(lambda own, number: shared_out(jax.random.fold_in(streams_of[1], 2), own, number, TGT_DEV * REQ, N_WIDE, 1, CAP, 2))(owner_of_keys, owner_of_turns).reshape((TARGETS, REQ, 1))
    row_of = plant(jax.random.randint(streams_of[2], (TARGETS, REQ), 0, NODE_DEV), jax.random.fold_in(streams_of[2], 1), 0, NODE_DEV - 1).astype(jnp.int32)
    w_self = bell_draw(streams_of[3], (F, H), (2 * F) ** -0.5, 0.15625, ((0, 4),))
    w_neighbor = bell_draw(streams_of[4], (F, H), (2 * F) ** -0.5, 0.15625, ((0, 4),))
    cotangent = bell_draw(streams_of[5], (TARGETS, H), (1.0 / TARGETS ** 0.5), 0.032958984, ((0, 256),))
    return dict(features=features, owner_of=owner_of, row_of=row_of, w_self=w_self, w_neighbor=w_neighbor, cotangent=cotangent)


def activation(value):
    return jax.nn.gelu(value, approximate=True)

def reference(features, owner_of, row_of, w_self, w_neighbor, cotangent):
    blocks = TARGETS // TGT_DEV
    owner_blocks = owner_of[:, :, 0].reshape(blocks, TGT_DEV, REQ)
    row_blocks = row_of.reshape(blocks, TGT_DEV, REQ)
    cot_blocks = cotangent.reshape(blocks, TGT_DEV, H)

    def step(carry, inputs):
        grad_s, grad_n = carry
        owners, rows, cots = inputs
        node = (owners * NODE_DEV + rows).astype(jnp.int32)
        gathered = jnp.transpose(jnp.take(features, node, axis=1), (1, 2, 0))
        self_rows = gathered[:, 0]
        pooled = (lax.optimization_barrier(jnp.sum(gathered[:, 1:].astype(jnp.float32), axis=1)) / FANOUT).astype(jnp.bfloat16)
        preact = jnp.dot(self_rows, w_self, preferred_element_type=jnp.float32) + jnp.dot(pooled, w_neighbor, preferred_element_type=jnp.float32)
        value, pullback = jax.vjp(activation, preact)
        slope = pullback(cots.astype(jnp.float32))[0].astype(jnp.bfloat16)
        grad_s = grad_s + jnp.dot(self_rows.T, slope, preferred_element_type=jnp.float32)
        grad_n = grad_n + jnp.dot(pooled.T, slope, preferred_element_type=jnp.float32)
        return ((grad_s, grad_n), value.astype(jnp.bfloat16))
    start = (jnp.zeros((F, H), jnp.float32), jnp.zeros((F, H), jnp.float32))
    (grad_self, grad_neighbor), hidden = lax.scan(step, start, (owner_blocks, row_blocks, cot_blocks))
    return (hidden.reshape(TARGETS, H), grad_self, grad_neighbor)
```

```python
import jax
import jax.numpy as jnp
from jax import lax
from jax.experimental import pallas as pl
from jax.experimental.pallas import tpu as pltpu
from jax.sharding import PartitionSpec as P

FANOUT = 15
NX, NY, NZ = 4, 4, 8
ROOT, CUBE = 0.7978845608, 0.044715


def remote(src, dst, send, recv, target):
    return pltpu.make_async_remote_copy(
        src_ref=src,
        dst_ref=dst,
        send_sem=send,
        recv_sem=recv,
        device_id=target,
        device_id_type=pl.DeviceIdType.MESH,
    )


def place():
    wide = lax.axis_index("wide")
    return wide // 16, lax.rem(wide // 2, 8), lax.rem(wide, 2), lax.axis_index("narrow")


def wide_at(y, z, core):
    return (y * 8 + z) * 2 + core


def greet(targets):
    barrier = pltpu.get_barrier_semaphore()
    for target in targets:
        pl.semaphore_signal(barrier, inc=1, device_id=target, device_id_type=pl.DeviceIdType.MESH)
    pl.semaphore_wait(barrier, len(targets))


def tail_kernel(
    rows_ref, w_ref, cot_ref, hid_ref, gs_ref, gn_ref,
    part, got_part, slopes, grads, got_core, got_z, got_y, full, final,
    x_send, x_recv, s_send, s_recv, c_send, c_recv, z_send, z_recv, y_send, y_recv, a_send, a_recv, d_send, d_recv,
):
    y, z, core, x = place()
    near_x = [{"wide": wide_at(y, z, core), "narrow": lax.rem(x + k, NX)} for k in range(1, NX)]
    near_c = {"wide": wide_at(y, z, 1 - core), "narrow": x}
    near_z = [{"wide": wide_at(y, lax.rem(z + k, NZ), core), "narrow": x} for k in range(1, NZ)]
    near_y = [{"wide": wide_at(lax.rem(y + k, NY), z, core), "narrow": x} for k in range(1, NY)]
    greet(near_x + [near_c] + near_z + near_y)

    for k in range(NX):
        part[k] = jnp.dot(rows_ref[k * 128:(k + 1) * 128], w_ref[...], preferred_element_type=jnp.float32)
    sent = []
    for k in range(1, NX):
        copy = remote(part.at[lax.rem(x + k, NX)], got_part.at[k - 1], x_send.at[k - 1], x_recv.at[k - 1], near_x[k - 1])
        copy.start()
        sent.append(copy)
    value = part[x]
    for k in range(1, NX):
        sent[k - 1].wait_recv()
        value = value + got_part[k - 1]
    bend = jnp.tanh(ROOT * (value + CUBE * value * value * value))
    hid_ref[...] = (0.5 * value * (1.0 + bend)).astype(jnp.bfloat16)
    rise = 0.5 * (1.0 + bend) + 0.5 * value * (1.0 - bend * bend) * ROOT * (1.0 + 3.0 * CUBE * value * value)
    slopes[x] = (cot_ref[...].astype(jnp.float32) * rise).astype(jnp.bfloat16)
    for k in range(1, NX):
        copy = remote(slopes.at[x], slopes.at[x], s_send.at[k - 1], s_recv.at[k - 1], near_x[k - 1])
        copy.start()
        sent.append(copy)
    for k in range(1, NX):
        remote(slopes.at[x], slopes.at[lax.rem(x + NX - k, NX)], s_send.at[k - 1], s_recv.at[k - 1], near_x[k - 1]).wait_recv()
    total = jnp.zeros((384, 256), jnp.float32)
    for k in range(NX):
        total = total + lax.dot_general(
            rows_ref[k * 128:(k + 1) * 128], slopes[k], (((0,), (0,)), ((), ())), preferred_element_type=jnp.float32
        )
    grads[...] = total.reshape(2, NZ, 24, 256)
    copy = remote(grads.at[1 - core], got_core, c_send, c_recv, near_c)
    copy.start()
    sent.append(copy)
    copy.wait_recv()
    full[core] = grads[core] + got_core[...]
    mine = full[core, z]
    for k in range(1, NZ):
        there = lax.rem(z + k, NZ)
        copy = remote(full.at[core, there], got_z.at[k - 1], z_send.at[k - 1], z_recv.at[k - 1], near_z[k - 1])
        copy.start()
        sent.append(copy)
    for k in range(1, NZ):
        remote(full.at[core, z], got_z.at[k - 1], z_send.at[k - 1], z_recv.at[k - 1], near_z[k - 1]).wait_recv()
        mine = mine + got_z[k - 1]
    got_y[y] = mine
    for k in range(1, NY):
        copy = remote(got_y.at[y], got_y.at[y], y_send.at[k - 1], y_recv.at[k - 1], near_y[k - 1])
        copy.start()
        sent.append(copy)
    for k in range(1, NY):
        remote(got_y.at[y], got_y.at[lax.rem(y + NY - k, NY)], y_send.at[k - 1], y_recv.at[k - 1], near_y[k - 1]).wait_recv()
    for copy in sent:
        copy.wait_send()
    final[core, z] = got_y[0] + got_y[1] + got_y[2] + got_y[3]
    last = []
    for k in range(1, NZ):
        copy = remote(final.at[core, z], final.at[core, z], a_send.at[k - 1], a_recv.at[k - 1], near_z[k - 1])
        copy.start()
        last.append(copy)
    for k in range(1, NZ):
        remote(final.at[core, z], final.at[core, lax.rem(z + NZ - k, NZ)], a_send.at[k - 1], a_recv.at[k - 1], near_z[k - 1]).wait_recv()
    copy = remote(final.at[core], final.at[core], d_send, d_recv, near_c)
    copy.start()
    last.append(copy)
    remote(final.at[core], final.at[1 - core], d_send, d_recv, near_c).wait_recv()
    for copy in last:
        copy.wait_send()
    whole = final[...].reshape(384, 256)
    gs_ref[...] = whole[:192]
    gn_ref[0:128] = whole[256:]
    gn_ref[128:192] = whole[192:256]


def tail(rows, weights, cotangent):
    vmem = pl.BlockSpec(memory_space=pltpu.VMEM)
    dma = pltpu.SemaphoreType.DMA
    return pl.pallas_call(
        tail_kernel,
        out_shape=(
            jax.ShapeDtypeStruct((128, 256), jnp.bfloat16),
            jax.ShapeDtypeStruct((192, 256), jnp.float32),
            jax.ShapeDtypeStruct((192, 256), jnp.float32),
        ),
        in_specs=[vmem] * 3,
        out_specs=(vmem, vmem, vmem),
        scratch_shapes=[
            pltpu.VMEM((NX, 128, 256), jnp.float32),
            pltpu.VMEM((NX - 1, 128, 256), jnp.float32),
            pltpu.VMEM((NX, 128, 256), jnp.bfloat16),
            pltpu.VMEM((2, NZ, 24, 256), jnp.float32),
            pltpu.VMEM((NZ, 24, 256), jnp.float32),
            pltpu.VMEM((NZ - 1, 24, 256), jnp.float32),
            pltpu.VMEM((NY, 24, 256), jnp.float32),
            pltpu.VMEM((2, NZ, 24, 256), jnp.float32),
            pltpu.VMEM((2, NZ, 24, 256), jnp.float32),
            dma((NX - 1,)), dma((NX - 1,)), dma((NX - 1,)), dma((NX - 1,)), dma(()), dma(()),
            dma((NZ - 1,)), dma((NZ - 1,)), dma((NY - 1,)), dma((NY - 1,)),
            dma((NZ - 1,)), dma((NZ - 1,)), dma(()), dma(()),
        ],
        compiler_params=pltpu.CompilerParams(collective_id=3, has_side_effects=True),
        name="tail",
    )(rows, weights, cotangent)


def slot_numbers(owners, wide_count, total):
    block_rows = 128
    block_count = total // block_rows
    onehot = (owners[:, None] == jnp.arange(wide_count, dtype=jnp.int32)[None, :]).astype(
        jnp.float32
    )
    blocked = onehot.reshape(block_count, block_rows, wide_count)
    lower = (jnp.arange(block_rows)[:, None] > jnp.arange(block_rows)[None, :]).astype(jnp.float32)
    within = jnp.einsum("ij,bjw->biw", lower, blocked, precision=lax.Precision.HIGHEST)
    block_sums = jnp.sum(blocked, axis=1)
    offsets = jnp.cumsum(block_sums, axis=0) - block_sums
    prefix = within + offsets[:, None, :]
    return jnp.sum(prefix * blocked, axis=2).reshape(total).astype(jnp.int32)


def on_device(features, owner_of, row_of, w_self, w_neighbor, cotangent):
    wide_count = lax.axis_size("wide")
    narrow_count = lax.axis_size("narrow")
    tgt_rows, request_count = row_of.shape
    feat_cols = features.shape[0]
    total = tgt_rows * request_count
    capacity = max(2, 3 * total // (2 * wide_count))
    owners = owner_of.reshape(total)
    wanted = row_of.reshape(total)
    slot_of = slot_numbers(owners, wide_count, total)
    flat_slot = owners * capacity + slot_of
    buffer = (
        jnp.zeros((wide_count * capacity,), jnp.int32)
        .at[flat_slot]
        .set(wanted)
        .reshape(wide_count, capacity)
    )
    table = jnp.transpose(features)
    found = jnp.take(
        table, lax.all_to_all(buffer, "wide", split_axis=0, concat_axis=0, tiled=True), axis=0
    )
    fetched = lax.all_to_all(found, "wide", split_axis=0, concat_axis=0, tiled=True)
    flat_fetched = fetched.reshape(wide_count * capacity, feat_cols)
    gathered = jnp.take(flat_fetched, flat_slot, axis=0).reshape(tgt_rows, request_count, feat_cols)
    self_rows = gathered[:, 0]
    pooled = (jnp.sum(gathered[:, 1:], axis=1, dtype=jnp.float32) / FANOUT).astype(jnp.bfloat16)
    rows = jnp.concatenate([self_rows, pooled[:, 128:], pooled[:, :128]], axis=1)
    weights = jnp.concatenate([w_self, w_neighbor[128:], w_neighbor[:128]], axis=0)
    return tail(rows, weights, cotangent)


def solution(mesh):
    return jax.shard_map(
        on_device,
        mesh=mesh,
        in_specs=(
            P("narrow", "wide"),
            P("wide", None, None),
            P("wide", None),
            P("narrow", None),
            P("narrow", None),
            P(("wide", "narrow"), None),
        ),
        out_specs=(P(("wide", "narrow"), None), P("narrow", None), P("narrow", None)),
        check_vma=False,
    )
```

```python
import jax
import jax.numpy as jnp
from jax import lax
from jax.experimental import pallas as pl
from jax.experimental.pallas import tpu as pltpu
from jax.sharding import PartitionSpec as P

FANOUT = 15
NX, NY, NZ = 4, 4, 8
ROOT, CUBE = 0.7978845608, 0.044715


def remote(src, dst, send, recv, target):
    return pltpu.make_async_remote_copy(
        src_ref=src,
        dst_ref=dst,
        send_sem=send,
        recv_sem=recv,
        device_id=target,
        device_id_type=pl.DeviceIdType.MESH,
    )


def place():
    wide = lax.axis_index("wide")
    return wide // 16, lax.rem(wide // 2, 8), lax.rem(wide, 2), lax.axis_index("narrow")


def wide_at(y, z, core):
    return (y * 8 + z) * 2 + core


def greet(targets):
    barrier = pltpu.get_barrier_semaphore()
    for target in targets:
        pl.semaphore_signal(barrier, inc=1, device_id=target, device_id_type=pl.DeviceIdType.MESH)
    pl.semaphore_wait(barrier, len(targets))


def tail_kernel(
    rows_ref, w_ref, cot_ref, hid_ref, gs_ref, gn_ref,
    part, got_part, slopes, grads, got_core, got_z, got_y, full, final,
    x_send, x_recv, s_send, s_recv, c_send, c_recv, z_send, z_recv, y_send, y_recv, a_send, a_recv, d_send, d_recv,
):
    y, z, core, x = place()
    near_x = [{"wide": wide_at(y, z, core), "narrow": lax.rem(x + k, NX)} for k in range(1, NX)]
    near_c = {"wide": wide_at(y, z, 1 - core), "narrow": x}
    near_z = [{"wide": wide_at(y, lax.rem(z + k, NZ), core), "narrow": x} for k in range(1, NZ)]
    near_y = [{"wide": wide_at(lax.rem(y + k, NY), z, core), "narrow": x} for k in range(1, NY)]
    greet(near_x + [near_c] + near_z + near_y)

    for k in range(NX):
        part[k] = jnp.dot(rows_ref[k * 128:(k + 1) * 128], w_ref[...], preferred_element_type=jnp.float32)
    sent = []
    for k in range(1, NX):
        copy = remote(part.at[lax.rem(x + k, NX)], got_part.at[k - 1], x_send.at[k - 1], x_recv.at[k - 1], near_x[k - 1])
        copy.start()
        sent.append(copy)
    value = part[x]
    for k in range(1, NX):
        sent[k - 1].wait_recv()
        value = value + got_part[k - 1]
    bend = jnp.tanh(ROOT * (value + CUBE * value * value * value))
    hid_ref[...] = (0.5 * value * (1.0 + bend)).astype(jnp.bfloat16)
    rise = 0.5 * (1.0 + bend) + 0.5 * value * (1.0 - bend * bend) * ROOT * (1.0 + 3.0 * CUBE * value * value)
    slopes[x] = (cot_ref[...].astype(jnp.float32) * rise).astype(jnp.bfloat16)
    for k in range(1, NX):
        copy = remote(slopes.at[x], slopes.at[x], s_send.at[k - 1], s_recv.at[k - 1], near_x[k - 1])
        copy.start()
        sent.append(copy)
    for k in range(1, NX):
        remote(slopes.at[x], slopes.at[lax.rem(x + NX - k, NX)], s_send.at[k - 1], s_recv.at[k - 1], near_x[k - 1]).wait_recv()
    total = jnp.zeros((384, 256), jnp.float32)
    for k in range(NX):
        total = total + lax.dot_general(
            rows_ref[k * 128:(k + 1) * 128], slopes[k], (((0,), (0,)), ((), ())), preferred_element_type=jnp.float32
        )
    grads[...] = total.reshape(2, NZ, 24, 256)
    copy = remote(grads.at[1 - core], got_core, c_send, c_recv, near_c)
    copy.start()
    sent.append(copy)
    copy.wait_recv()
    full[core] = grads[core] + got_core[...]
    mine = full[core, z]
    for k in range(1, NZ):
        there = lax.rem(z + k, NZ)
        copy = remote(full.at[core, there], got_z.at[k - 1], z_send.at[k - 1], z_recv.at[k - 1], near_z[k - 1])
        copy.start()
        sent.append(copy)
    for k in range(1, NZ):
        remote(full.at[core, z], got_z.at[k - 1], z_send.at[k - 1], z_recv.at[k - 1], near_z[k - 1]).wait_recv()
        mine = mine + got_z[k - 1]
    got_y[y] = mine
    for k in range(1, NY):
        copy = remote(got_y.at[y], got_y.at[y], y_send.at[k - 1], y_recv.at[k - 1], near_y[k - 1])
        copy.start()
        sent.append(copy)
    for k in range(1, NY):
        remote(got_y.at[y], got_y.at[lax.rem(y + NY - k, NY)], y_send.at[k - 1], y_recv.at[k - 1], near_y[k - 1]).wait_recv()
    for copy in sent:
        copy.wait_send()
    final[core, z] = got_y[0] + got_y[1] + got_y[2] + got_y[3]
    last = []
    for k in range(1, NZ):
        copy = remote(final.at[core, z], final.at[core, z], a_send.at[k - 1], a_recv.at[k - 1], near_z[k - 1])
        copy.start()
        last.append(copy)
    for k in range(1, NZ):
        remote(final.at[core, z], final.at[core, lax.rem(z + NZ - k, NZ)], a_send.at[k - 1], a_recv.at[k - 1], near_z[k - 1]).wait_recv()
    copy = remote(final.at[core], final.at[core], d_send, d_recv, near_c)
    copy.start()
    last.append(copy)
    remote(final.at[core], final.at[1 - core], d_send, d_recv, near_c).wait_recv()
    for copy in last:
        copy.wait_send()
    whole = final[...].reshape(384, 256)
    gs_ref[...] = whole[:192]
    gn_ref[0:128] = whole[256:]
    gn_ref[128:192] = whole[192:256]


def tail(rows, weights, cotangent):
    vmem = pl.BlockSpec(memory_space=pltpu.VMEM)
    dma = pltpu.SemaphoreType.DMA
    return pl.pallas_call(
        tail_kernel,
        out_shape=(
            jax.ShapeDtypeStruct((128, 256), jnp.bfloat16),
            jax.ShapeDtypeStruct((192, 256), jnp.float32),
            jax.ShapeDtypeStruct((192, 256), jnp.float32),
        ),
        in_specs=[vmem] * 3,
        out_specs=(vmem, vmem, vmem),
        scratch_shapes=[
            pltpu.VMEM((NX, 128, 256), jnp.float32),
            pltpu.VMEM((NX - 1, 128, 256), jnp.float32),
            pltpu.VMEM((NX, 128, 256), jnp.bfloat16),
            pltpu.VMEM((2, NZ, 24, 256), jnp.float32),
            pltpu.VMEM((NZ, 24, 256), jnp.float32),
            pltpu.VMEM((NZ - 1, 24, 256), jnp.float32),
            pltpu.VMEM((NY, 24, 256), jnp.float32),
            pltpu.VMEM((2, NZ, 24, 256), jnp.float32),
            pltpu.VMEM((2, NZ, 24, 256), jnp.float32),
            dma((NX - 1,)), dma((NX - 1,)), dma((NX - 1,)), dma((NX - 1,)), dma(()), dma(()),
            dma((NZ - 1,)), dma((NZ - 1,)), dma((NY - 1,)), dma((NY - 1,)),
            dma((NZ - 1,)), dma((NZ - 1,)), dma(()), dma(()),
        ],
        compiler_params=pltpu.CompilerParams(collective_id=3, has_side_effects=True),
        name="tail",
    )(rows, weights, cotangent)


def order_of(step):
    odd = lax.rem(step, 2)
    return jnp.where(step == 0, 4, jnp.where(odd == 1, 3 - step // 2, 4 + step // 2))


def list_requests(own_ref, row_ref, listed):
    upper = (
        lax.broadcasted_iota(jnp.int32, (512, 512), 0) < lax.broadcasted_iota(jnp.int32, (512, 512), 1)
    ).astype(jnp.float32).astype(jnp.bfloat16)
    owner_id = lax.broadcasted_iota(jnp.int32, (64, 512), 0)
    slot_id = lax.broadcasted_iota(jnp.int32, (256, 512), 0)
    slot_id = jnp.where(slot_id < 192, slot_id, slot_id - 64)
    lane = lax.broadcasted_iota(jnp.int32, (1, 512), 1)

    def one(j, carry):
        used, found = carry
        owner = own_ref[j]
        row = row_ref[pl.ds(j, 1), :]
        place_of = ((owner >> 1) & 7) * 8 + (owner >> 4) * 2 + (owner & 1)
        mine = owner_id == place_of
        onehot = jnp.where(mine, 1.0, 0.0)
        within = jnp.dot(onehot.astype(jnp.bfloat16), upper, preferred_element_type=jnp.float32)
        slot = jnp.sum(onehot * (within + used), axis=0, keepdims=True).astype(jnp.int32)
        spot = jnp.where(slot_id == slot, 1.0, 0.0).astype(jnp.bfloat16)
        pieces = [row & 255, row >> 8, lane & 255, (lane >> 8) + 2 * j + 1]
        stacked = jnp.concatenate(
            [jnp.where(mine, piece.astype(jnp.float32), 0.0) for piece in pieces], axis=0
        ).astype(jnp.bfloat16)
        found = found + lax.dot_general(
            stacked, spot, (((1,), (1,)), ((), ())), preferred_element_type=jnp.float32
        )
        return used + jnp.sum(onehot, axis=1, keepdims=True), found

    _, found = lax.fori_loop(
        0, 16, one, (jnp.zeros((64, 1), jnp.float32), jnp.zeros((256, 256), jnp.float32))
    )
    found = found.astype(jnp.int32)
    row = found[0:64] + 256 * found[64:128]
    block = found[192:256]
    item = found[128:192] + 256 * (block - 1)
    target = jnp.where(block > 0, jnp.where(item < 512, item, 512 + (item & 511)), 1024)
    listed[...] = (row + 8192 * target).reshape(8, 8, 256)


def front_kernel(
    feat_ref, own_ref, row_ref, out_ref,
    listed, via, turned, asked, rows_of, index, dest, table, near, outgoing, landed, choose, held, dense, ring, ringed,
    a_send, a_recv, b_send, b_recv, i_sem, f_send, f_recv, o_sem, r_send, r_recv,
):
    y, z, core, x = place()
    near_z = [{"wide": wide_at(y, lax.rem(z + k, NZ), core), "narrow": x} for k in range(1, NZ)]

    def plane(q):
        return lax.rem(y + q // 2, NY), lax.rem(core + q, 2)

    def plane_at(q):
        there, seat = plane(q)
        return {"wide": wide_at(there, z, seat), "narrow": x}

    greet(near_z + [plane_at(q) for q in range(1, 8)])
    me = y * 2 + core

    list_requests(own_ref, row_ref, listed)
    for k in range(1, NZ):
        remote(listed.at[lax.rem(z + k, NZ)], via.at[z], a_send.at[k - 1], a_recv.at[k - 1], near_z[k - 1]).start()
    via[z] = listed[z]

    eye = (
        lax.broadcasted_iota(jnp.int32, (256, 256), 0) == lax.broadcasted_iota(jnp.int32, (256, 256), 1)
    ).astype(jnp.float32).astype(jnp.bfloat16)

    def turn(b, _):
        start = pl.multiple_of(b * 256, 256)
        block = feat_ref[:, pl.ds(start, 256)]
        block = jnp.concatenate([block, block[128:]], axis=0)
        table[pl.ds(start, 256), :] = lax.dot_general(
            eye, block, (((1,), (1,)), ((), ())), preferred_element_type=jnp.float32
        )
        return 0

    lax.fori_loop(0, 16, turn, 0)
    for k in range(1, NZ):
        remote(listed.at[z], via.at[lax.rem(z + NZ - k, NZ)], a_send.at[k - 1], a_recv.at[k - 1], near_z[k - 1]).wait_recv()
    for group in range(8):
        for owner in range(8):
            turned[owner, group:group + 1] = via[group, owner:owner + 1]

    def tell(q, _):
        there, seat = plane(q)
        remote(turned.at[there * 2 + seat], asked.at[me], b_send.at[q], b_recv.at[q], plane_at(q)).start()
        return 0

    lax.fori_loop(1, 8, tell, 0)
    asked[me] = turned[me]
    for owner in range(8):
        dest[:, owner * 192:(owner + 1) * 192] = turned[owner][:, :192] >> 13
    lax.fori_loop(16, 32, turn, 0)

    def told(q, _):
        remote(turned.at[0], asked.at[0], b_send.at[q], b_recv.at[q], plane_at(q)).wait_recv()
        return 0

    lax.fori_loop(1, 8, told, 0)
    rows_of[...] = (asked[...] & 8191).reshape(64, 256)
    copy = pltpu.make_async_copy(rows_of, index, i_sem)
    copy.start()
    copy.wait()

    low_half = lax.broadcasted_iota(jnp.int32, (96, 128), 1) < 64
    low_lane = lax.broadcasted_iota(jnp.int32, (512, 128), 1) < 64

    def fetch(step):
        group = lax.rem(z + order_of(step), NZ)

        def one(q, _):
            there, seat = plane(q)
            line = (there * 2 + seat) * 8 + group

            def pick(s, _):
                for u in range(8):
                    node = index[line, s * 8 + u]
                    near[s, u:u + 1, :] = table[pl.ds(node, 1), :]
                return 0

            lax.fori_loop(0, 24, pick, 0)
            wide_rows = near[...].reshape(192, 256)
            outgoing[step, q, 0:192] = wide_rows[:, :128].astype(jnp.bfloat16)
            outgoing[step, q, 192:288] = jnp.where(low_half, wide_rows[:96, 128:], wide_rows[96:, 128:]).astype(jnp.bfloat16)

            @pl.when(q > 0)
            def _():
                remote(outgoing.at[step, q], landed.at[step, me], f_send.at[step, q], f_recv.at[step, q], plane_at(q)).start()

            @pl.when(q == 0)
            def _():
                pltpu.make_async_copy(outgoing.at[step, q], landed.at[step, me], o_sem.at[step]).start()

            return 0

        lax.fori_loop(0, 8, one, 0)

    def gather_in(step):
        group = lax.rem(z + order_of(step), NZ)
        target_id = lax.broadcasted_iota(jnp.int32, (1024, 256), 0)
        for b in range(6):
            choose[:, b * 256:(b + 1) * 256] = jnp.where(
                target_id == dest[pl.ds(group, 1), b * 256:(b + 1) * 256], 1.0, 0.0
            ).astype(jnp.bfloat16)
        pltpu.make_async_copy(outgoing.at[step, 0], landed.at[step, me], o_sem.at[step]).wait()

        def got(q, _):
            remote(outgoing.at[step, q], landed.at[step, me], f_send.at[step, q], f_recv.at[step, q], plane_at(q)).wait_recv()
            return 0

        lax.fori_loop(1, 8, got, 0)
        for owner in range(8):
            base = owner * 192
            held[base:base + 192, 0:128] = landed[step, owner, 0:192]
            pair = landed[step, owner, 192:288]
            held[base:base + 96, 128:256] = pair
            held[base + 96:base + 192, 128:256] = pltpu.roll(pair.astype(jnp.float32), 64, 1).astype(jnp.bfloat16)
        for part in range(4):
            dense[part * 256:(part + 1) * 256] = jnp.dot(
                choose[part * 256:(part + 1) * 256], held[...], preferred_element_type=jnp.float32
            )

    def pieces():
        mixed = jnp.where(low_lane, dense[0:512, 128:256], pltpu.roll(dense[512:1024, 128:256], 64, 1))
        return [dense[0:512, 0:128], mixed, dense[512:1024, 0:128]]

    def ring_at(step):
        up = jnp.logical_or(step == 0, lax.rem(step, 2) == 1)
        return {"wide": wide_at(y, lax.rem(z + jnp.where(up, 1, NZ - 1), NZ), core), "narrow": x}

    def ring_copy(step):
        return remote(ring.at[step], ringed.at[step], r_send.at[step], r_recv.at[step], ring_at(step))

    def pass_on(step):
        @pl.when(jnp.logical_or(step == 0, step == 2))
        def _():
            for i, piece in enumerate(pieces()):
                ring[step, i] = piece.astype(jnp.bfloat16)

        @pl.when(jnp.logical_and(step != 0, step != 2))
        def _():
            before = jnp.where(step == 1, 0, step - 2)
            ring_copy(before).wait_recv()
            for i, piece in enumerate(pieces()):
                ring[step, i] = (piece + ringed[before, i].astype(jnp.float32)).astype(jnp.bfloat16)

        ring_copy(step).start()

    fetch(0)

    def loop(step, _):
        fetch(step + 1)
        gather_in(step)
        pass_on(step)
        return 0

    lax.fori_loop(0, 7, loop, 0)
    gather_in(7)
    ring_copy(5).wait_recv()
    ring_copy(6).wait_recv()
    for i, piece in enumerate(pieces()):
        total = piece + ringed[5, i].astype(jnp.float32) + ringed[6, i].astype(jnp.float32)
        if i == 1:
            total = jnp.where(low_lane, total, total / FANOUT)
        if i == 2:
            total = total / FANOUT
        out_ref[:, i * 128:(i + 1) * 128] = total.astype(jnp.bfloat16)

    for k in range(1, NZ):
        remote(listed.at[z], via.at[z], a_send.at[k - 1], a_recv.at[k - 1], near_z[k - 1]).wait_send()

    def drain(q, _):
        remote(turned.at[0], asked.at[0], b_send.at[q], b_recv.at[q], plane_at(q)).wait_send()

        def each(step, _):
            remote(outgoing.at[step, q], landed.at[step, me], f_send.at[step, q], f_recv.at[step, q], plane_at(q)).wait_send()
            return 0

        lax.fori_loop(0, 8, each, 0)
        return 0

    lax.fori_loop(1, 8, drain, 0)

    def drain_ring(step, _):
        ring_copy(step).wait_send()
        return 0

    lax.fori_loop(0, 7, drain_ring, 0)


def front(features, owner_of, row_of):
    vmem = pl.BlockSpec(memory_space=pltpu.VMEM)
    dma = pltpu.SemaphoreType.DMA
    return pl.pallas_call(
        front_kernel,
        out_shape=jax.ShapeDtypeStruct((512, 384), jnp.bfloat16),
        in_specs=[vmem] * 3,
        out_specs=vmem,
        scratch_shapes=[
            pltpu.VMEM((8, 8, 256), jnp.int32),
            pltpu.VMEM((8, 8, 256), jnp.int32),
            pltpu.VMEM((8, 8, 256), jnp.int32),
            pltpu.VMEM((8, 8, 256), jnp.int32),
            pltpu.VMEM((64, 256), jnp.int32),
            pltpu.SMEM((64, 256), jnp.int32),
            pltpu.VMEM((8, 1536), jnp.int32),
            pltpu.VMEM((8192, 256), jnp.float32),
            pltpu.VMEM((24, 8, 256), jnp.float32),
            pltpu.VMEM((8, 8, 288, 128), jnp.bfloat16),
            pltpu.VMEM((8, 8, 288, 128), jnp.bfloat16),
            pltpu.VMEM((1024, 1536), jnp.bfloat16),
            pltpu.VMEM((1536, 256), jnp.bfloat16),
            pltpu.VMEM((1024, 256), jnp.float32),
            pltpu.VMEM((7, 3, 512, 128), jnp.bfloat16),
            pltpu.VMEM((7, 3, 512, 128), jnp.bfloat16),
            dma((NZ - 1,)), dma((NZ - 1,)), dma((8,)), dma((8,)), dma(()),
            dma((8, 8)), dma((8, 8)), dma((8,)), dma((7,)), dma((7,)),
        ],
        compiler_params=pltpu.CompilerParams(
            collective_id=1, has_side_effects=True, vmem_limit_bytes=60 * 1024 * 1024
        ),
        name="front",
    )(features, jnp.transpose(owner_of, (1, 2, 0)), jnp.transpose(row_of))


def on_device(features, owner_of, row_of, w_self, w_neighbor, cotangent):
    rows = front(features, owner_of, row_of)
    weights = jnp.concatenate([w_self, w_neighbor[128:], w_neighbor[:128]], axis=0)
    return tail(rows, weights, cotangent)


def solution(mesh):
    return jax.shard_map(
        on_device,
        mesh=mesh,
        in_specs=(
            P("narrow", "wide"),
            P("wide", None, None),
            P("wide", None),
            P("narrow", None),
            P("narrow", None),
            P(("wide", "narrow"), None),
        ),
        out_specs=(P(("wide", "narrow"), None), P("narrow", None), P("narrow", None)),
        check_vma=False,
    )
```

```python
import jax
import jax.numpy as jnp
from jax import lax
from jax.experimental import pallas as pl
from jax.experimental.pallas import tpu as pltpu
from jax.sharding import PartitionSpec as P

FANOUT = 15
NX, NY, NZ = 4, 4, 8
ROOT, CUBE = 0.7978845608, 0.044715


def remote(src, dst, send, recv, target):
    return pltpu.make_async_remote_copy(
        src_ref=src,
        dst_ref=dst,
        send_sem=send,
        recv_sem=recv,
        device_id=target,
        device_id_type=pl.DeviceIdType.MESH,
    )


def place():
    wide = lax.axis_index("wide")
    return wide // 16, lax.rem(wide // 2, 8), lax.rem(wide, 2), lax.axis_index("narrow")


def wide_at(y, z, core):
    return (y * 8 + z) * 2 + core


def order_of(step):
    odd = lax.rem(step, 2)
    return jnp.where(step == 0, 4, jnp.where(odd == 1, 3 - step // 2, 4 + step // 2))


def list_requests(own_ref, row_ref, listed):
    upper = (
        lax.broadcasted_iota(jnp.int32, (512, 512), 0) < lax.broadcasted_iota(jnp.int32, (512, 512), 1)
    ).astype(jnp.float32).astype(jnp.bfloat16)
    owner_id = lax.broadcasted_iota(jnp.int32, (64, 512), 0)
    slot_id = lax.broadcasted_iota(jnp.int32, (256, 512), 0)
    slot_id = jnp.where(slot_id < 192, slot_id, slot_id - 64)
    lane = lax.broadcasted_iota(jnp.int32, (1, 512), 1)

    def one(j, carry):
        used, found = carry
        owner = own_ref[j]
        row = row_ref[pl.ds(j, 1), :]
        place_of = ((owner >> 1) & 7) * 8 + (owner >> 4) * 2 + (owner & 1)
        mine = owner_id == place_of
        onehot = jnp.where(mine, 1.0, 0.0)
        within = jnp.dot(onehot.astype(jnp.bfloat16), upper, preferred_element_type=jnp.float32)
        slot = jnp.sum(onehot * (within + used), axis=0, keepdims=True).astype(jnp.int32)
        spot = jnp.where(slot_id == slot, 1.0, 0.0).astype(jnp.bfloat16)
        pieces = [row & 255, row >> 8, lane & 255, (lane >> 8) + 2 * j + 1]
        stacked = jnp.concatenate(
            [jnp.where(mine, piece.astype(jnp.float32), 0.0) for piece in pieces], axis=0
        ).astype(jnp.bfloat16)
        found = found + lax.dot_general(
            stacked, spot, (((1,), (1,)), ((), ())), preferred_element_type=jnp.float32
        )
        return used + jnp.sum(onehot, axis=1, keepdims=True), found

    _, found = lax.fori_loop(
        0, 16, one, (jnp.zeros((64, 1), jnp.float32), jnp.zeros((256, 256), jnp.float32))
    )
    found = found.astype(jnp.int32)
    row = found[0:64] + 256 * found[64:128]
    block = found[192:256]
    item = found[128:192] + 256 * (block - 1)
    target = jnp.where(block > 0, jnp.where(item < 512, item, 512 + (item & 511)), 1024)
    listed[...] = (row + 8192 * target).reshape(8, 8, 256)


def step_kernel(
    feat_ref, own_ref, row_ref, ws_ref, wn_ref, cot_ref, hid_ref, final,
    feat, listed, via, turned, asked, rows_of, index, dest, table, near, outgoing, landed, choose, held, dense, ring, ringed,
    rows, part, part_out, got_part, slopes, grads, got_core, full, full_out, got_z, got_y,
    e_sem, a_send, a_recv, b_send, b_recv, i_sem, f_send, f_recv, o_sem, r_send, r_recv,
    x_send, x_recv, s_send, s_recv, c_send, c_recv, z_send, z_recv, y_send, y_recv, g_send, g_recv, d_send, d_recv,
):
    y, z, core, x = place()
    near_z = [{"wide": wide_at(y, lax.rem(z + k, NZ), core), "narrow": x} for k in range(1, NZ)]
    near_x = [{"wide": wide_at(y, z, core), "narrow": lax.rem(x + k, NX)} for k in range(1, NX)]

    def plane(q):
        return lax.rem(y + q // 2, NY), lax.rem(core + q, 2)

    def plane_at(q):
        there, seat = plane(q)
        return {"wide": wide_at(there, z, seat), "narrow": x}

    barrier = pltpu.get_barrier_semaphore()
    targets = near_z + [plane_at(q) for q in range(1, 8)] + near_x
    for target in targets:
        pl.semaphore_signal(barrier, inc=1, device_id=target, device_id_type=pl.DeviceIdType.MESH)
    feat_copy = pltpu.make_async_copy(feat_ref, feat, e_sem)
    feat_copy.start()
    me = y * 2 + core

    list_requests(own_ref, row_ref, listed)
    pl.semaphore_wait(barrier, len(targets))
    for k in range(1, NZ):
        remote(listed.at[lax.rem(z + k, NZ)], via.at[z], a_send.at[k - 1], a_recv.at[k - 1], near_z[k - 1]).start()
    via[z] = listed[z]

    eye = (
        lax.broadcasted_iota(jnp.int32, (256, 256), 0) == lax.broadcasted_iota(jnp.int32, (256, 256), 1)
    ).astype(jnp.float32).astype(jnp.bfloat16)

    def turn(b, _):
        start = pl.multiple_of(b * 256, 256)
        block = feat[:, pl.ds(start, 256)]
        block = jnp.concatenate([block, block[128:]], axis=0)
        turned_block = lax.dot_general(eye, block, (((1,), (1,)), ((), ())), preferred_element_type=jnp.float32)
        table[pl.ds(2 * start, 256, stride=2), :] = turned_block[:, :128]
        table[pl.ds(2 * start + 1, 256, stride=2), :] = turned_block[:, 128:]
        return 0

    feat_copy.wait()
    lax.fori_loop(0, 16, turn, 0)
    for k in range(1, NZ):
        remote(listed.at[z], via.at[lax.rem(z + NZ - k, NZ)], a_send.at[k - 1], a_recv.at[k - 1], near_z[k - 1]).wait_recv()
    for group in range(8):
        for owner in range(8):
            turned[owner, group:group + 1] = via[group, owner:owner + 1]

    def tell(q, _):
        there, seat = plane(q)
        remote(turned.at[there * 2 + seat], asked.at[me], b_send.at[q], b_recv.at[q], plane_at(q)).start()
        return 0

    lax.fori_loop(1, 8, tell, 0)
    asked[me] = turned[me]
    for owner in range(8):
        dest[:, owner * 192:(owner + 1) * 192] = turned[owner][:, :192] >> 13
    lax.fori_loop(16, 32, turn, 0)

    def told(q, _):
        remote(turned.at[0], asked.at[0], b_send.at[q], b_recv.at[q], plane_at(q)).wait_recv()
        return 0

    lax.fori_loop(1, 8, told, 0)
    rows_of[...] = 2 * (asked[...] & 8191).reshape(64, 256)
    copy = pltpu.make_async_copy(rows_of, index, i_sem)
    copy.start()
    copy.wait()

    low_half = lax.broadcasted_iota(jnp.int32, (96, 128), 1) < 64
    low_lane = lax.broadcasted_iota(jnp.int32, (512, 128), 1) < 64

    def fetch(step):
        group = lax.rem(z + order_of(step), NZ)

        def one(q, _):
            there, seat = plane(q)
            line = (there * 2 + seat) * 8 + group

            for s in range(192):
                near[2 * s:2 * s + 2, :] = table[pl.ds(index[line, s], 2), :]
            outgoing[step, q, 0:192] = near[pl.ds(0, 192, stride=2), :].astype(jnp.bfloat16)
            outgoing[step, q, 192:288] = jnp.where(
                low_half, near[pl.ds(1, 96, stride=2), :], near[pl.ds(193, 96, stride=2), :]
            ).astype(jnp.bfloat16)

            @pl.when(q > 0)
            def _():
                remote(outgoing.at[step, q], landed.at[step, me], f_send.at[step, q], f_recv.at[step, q], plane_at(q)).start()

            @pl.when(q == 0)
            def _():
                pltpu.make_async_copy(outgoing.at[step, q], landed.at[step, me], o_sem.at[step]).start()

            return 0

        lax.fori_loop(0, 8, one, 0)

    def gather_in(step):
        group = lax.rem(z + order_of(step), NZ)
        target_id = lax.broadcasted_iota(jnp.int32, (1024, 256), 0)
        for b in range(6):
            choose[:, b * 256:(b + 1) * 256] = jnp.where(
                target_id == dest[pl.ds(group, 1), b * 256:(b + 1) * 256], 1.0, 0.0
            ).astype(jnp.bfloat16)
        pltpu.make_async_copy(outgoing.at[step, 0], landed.at[step, me], o_sem.at[step]).wait()

        def got(q, _):
            remote(outgoing.at[step, q], landed.at[step, me], f_send.at[step, q], f_recv.at[step, q], plane_at(q)).wait_recv()
            return 0

        lax.fori_loop(1, 8, got, 0)
        for owner in range(8):
            base = owner * 192
            held[base:base + 192, 0:128] = landed[step, owner, 0:192]
            pair = landed[step, owner, 192:288]
            held[base:base + 96, 128:256] = pair
            held[base + 96:base + 192, 128:256] = pltpu.roll(pair.astype(jnp.float32), 64, 1).astype(jnp.bfloat16)
        for part in range(4):
            dense[part * 256:(part + 1) * 256] = jnp.dot(
                choose[part * 256:(part + 1) * 256], held[...], preferred_element_type=jnp.float32
            )

    def pieces():
        mixed = jnp.where(low_lane, dense[0:512, 128:256], pltpu.roll(dense[512:1024, 128:256], 64, 1))
        return [dense[0:512, 0:128], mixed, dense[512:1024, 0:128]]

    def ring_at(step):
        up = jnp.logical_or(step == 0, lax.rem(step, 2) == 1)
        return {"wide": wide_at(y, lax.rem(z + jnp.where(up, 1, NZ - 1), NZ), core), "narrow": x}

    def ring_copy(step):
        return remote(ring.at[step], ringed.at[step], r_send.at[step], r_recv.at[step], ring_at(step))

    def pass_on(step):
        @pl.when(jnp.logical_or(step == 0, step == 2))
        def _():
            for i, piece in enumerate(pieces()):
                ring[step, i] = piece.astype(jnp.bfloat16)

        @pl.when(jnp.logical_and(step != 0, step != 2))
        def _():
            before = jnp.where(step == 1, 0, step - 2)
            ring_copy(before).wait_recv()
            for i, piece in enumerate(pieces()):
                ring[step, i] = (piece + ringed[before, i].astype(jnp.float32)).astype(jnp.bfloat16)

        ring_copy(step).start()

    fetch(0)

    def loop(step, _):
        fetch(step + 1)
        gather_in(step)
        pass_on(step)
        return 0

    lax.fori_loop(0, 7, loop, 0)
    gather_in(7)
    ring_copy(5).wait_recv()
    ring_copy(6).wait_recv()
    for i, piece in enumerate(pieces()):
        total = piece + ringed[5, i].astype(jnp.float32) + ringed[6, i].astype(jnp.float32)
        if i == 1:
            total = jnp.where(low_lane, total, total / FANOUT)
        if i == 2:
            total = total / FANOUT
        rows[:, i * 128:(i + 1) * 128] = total.astype(jnp.bfloat16)

    middle = jnp.concatenate([ws_ref[128:192], wn_ref[128:192]], axis=0)
    for k in range(NX):
        span = slice(k * 128, (k + 1) * 128)
        value = jnp.dot(rows[span, 0:128], ws_ref[0:128], preferred_element_type=jnp.float32)
        value = value + jnp.dot(rows[span, 128:256], middle, preferred_element_type=jnp.float32)
        value = value + jnp.dot(rows[span, 256:384], wn_ref[0:128], preferred_element_type=jnp.float32)
        part[k] = value
        part_out[k] = value.astype(jnp.bfloat16)
    sent = []
    for k in range(1, NX):
        copy = remote(part_out.at[lax.rem(x + k, NX)], got_part.at[k - 1], x_send.at[k - 1], x_recv.at[k - 1], near_x[k - 1])
        copy.start()
        sent.append(copy)
    value = part[x]
    for k in range(1, NX):
        sent[k - 1].wait_recv()
        value = value + got_part[k - 1].astype(jnp.float32)
    bend = jnp.tanh(ROOT * (value + CUBE * value * value * value))
    rise = 0.5 * (1.0 + bend) + 0.5 * value * (1.0 - bend * bend) * ROOT * (1.0 + 3.0 * CUBE * value * value)
    slopes[x] = (cot_ref[...].astype(jnp.float32) * rise).astype(jnp.bfloat16)
    for k in range(1, NX):
        copy = remote(slopes.at[x], slopes.at[x], s_send.at[k - 1], s_recv.at[k - 1], near_x[k - 1])
        copy.start()
        sent.append(copy)
    hid_ref[...] = (0.5 * value * (1.0 + bend)).astype(jnp.bfloat16)
    for k in range(1, NX):
        remote(slopes.at[x], slopes.at[lax.rem(x + NX - k, NX)], s_send.at[k - 1], s_recv.at[k - 1], near_x[k - 1]).wait_recv()
    grads[...] = lax.dot_general(
        rows[...], slopes[...].reshape(512, 256), (((0,), (0,)), ((), ())), preferred_element_type=jnp.float32
    ).reshape(2, NZ, 24, 256)
    copy = remote(grads.at[1 - core], got_core, c_send, c_recv, plane_at(1))
    copy.start()
    sent.append(copy)
    copy.wait_recv()
    full[...] = grads[core] + got_core[...]
    full_out[...] = full[...].astype(jnp.bfloat16)
    for k in range(1, NZ):
        copy = remote(full_out.at[lax.rem(z + k, NZ)], got_z.at[k - 1], z_send.at[k - 1], z_recv.at[k - 1], near_z[k - 1])
        copy.start()
        sent.append(copy)
    mine = full[z]
    for k in range(1, NZ):
        remote(full_out.at[z], got_z.at[k - 1], z_send.at[k - 1], z_recv.at[k - 1], near_z[k - 1]).wait_recv()
        mine = mine + got_z[k - 1].astype(jnp.float32)
    got_y[y] = mine
    for k in range(1, NY):
        copy = remote(got_y.at[y], got_y.at[y], y_send.at[k - 1], y_recv.at[k - 1], plane_at(2 * k))
        copy.start()
        sent.append(copy)
    for k in range(1, NY):
        remote(got_y.at[y], got_y.at[lax.rem(y + NY - k, NY)], y_send.at[k - 1], y_recv.at[k - 1], plane_at(2 * k)).wait_recv()
    final[core, z] = (got_y[0] + got_y[1] + got_y[2] + got_y[3]).astype(jnp.bfloat16)
    for k in range(1, NZ):
        copy = remote(final.at[core, z], final.at[core, z], g_send.at[k - 1], g_recv.at[k - 1], near_z[k - 1])
        copy.start()
        sent.append(copy)
    for k in range(1, NZ):
        remote(final.at[core, z], final.at[core, lax.rem(z + NZ - k, NZ)], g_send.at[k - 1], g_recv.at[k - 1], near_z[k - 1]).wait_recv()
    copy = remote(final.at[core], final.at[core], d_send, d_recv, plane_at(1))
    copy.start()
    sent.append(copy)
    remote(final.at[core], final.at[1 - core], d_send, d_recv, plane_at(1)).wait_recv()
    for copy in sent:
        copy.wait_send()

    for k in range(1, NZ):
        remote(listed.at[z], via.at[z], a_send.at[k - 1], a_recv.at[k - 1], near_z[k - 1]).wait_send()

    def drain(q, _):
        remote(turned.at[0], asked.at[0], b_send.at[q], b_recv.at[q], plane_at(q)).wait_send()

        def each(step, _):
            remote(outgoing.at[step, q], landed.at[step, me], f_send.at[step, q], f_recv.at[step, q], plane_at(q)).wait_send()
            return 0

        lax.fori_loop(0, 8, each, 0)
        return 0

    lax.fori_loop(1, 8, drain, 0)

    def drain_ring(step, _):
        ring_copy(step).wait_send()
        return 0

    lax.fori_loop(0, 7, drain_ring, 0)


def finish_kernel(hid_ref, final_ref, out_ref, gs_ref, gn_ref):
    out_ref[...] = hid_ref[...]
    whole = final_ref[...].astype(jnp.float32).reshape(384, 256)
    gs_ref[...] = whole[:192]
    gn_ref[0:128] = whole[256:]
    gn_ref[128:192] = whole[192:256]


def on_device(features, owner_of, row_of, w_self, w_neighbor, cotangent):
    vmem = pl.BlockSpec(memory_space=pltpu.VMEM)
    dma = pltpu.SemaphoreType.DMA
    f32, bf16, i32 = jnp.float32, jnp.bfloat16, jnp.int32
    hidden, final = pl.pallas_call(
        step_kernel,
        out_shape=(jax.ShapeDtypeStruct((128, 256), bf16), jax.ShapeDtypeStruct((2, NZ, 24, 256), bf16)),
        in_specs=[pl.BlockSpec(memory_space=pl.ANY)] + [vmem] * 5,
        out_specs=(vmem, vmem),
        scratch_shapes=[
            pltpu.VMEM((192, 8192), bf16),
            pltpu.VMEM((8, 8, 256), i32),
            pltpu.VMEM((8, 8, 256), i32),
            pltpu.VMEM((8, 8, 256), i32),
            pltpu.VMEM((8, 8, 256), i32),
            pltpu.VMEM((64, 256), i32),
            pltpu.SMEM((64, 256), i32),
            pltpu.VMEM((8, 1536), i32),
            pltpu.VMEM((16384, 128), f32),
            pltpu.VMEM((384, 128), f32),
            pltpu.VMEM((8, 8, 288, 128), bf16),
            pltpu.VMEM((8, 8, 288, 128), bf16),
            pltpu.VMEM((1024, 1536), bf16),
            pltpu.VMEM((1536, 256), bf16),
            pltpu.VMEM((1024, 256), f32),
            pltpu.VMEM((7, 3, 512, 128), bf16),
            pltpu.VMEM((7, 3, 512, 128), bf16),
            pltpu.VMEM((512, 384), bf16),
            pltpu.VMEM((NX, 128, 256), f32),
            pltpu.VMEM((NX, 128, 256), bf16),
            pltpu.VMEM((NX - 1, 128, 256), bf16),
            pltpu.VMEM((NX, 128, 256), bf16),
            pltpu.VMEM((2, NZ, 24, 256), f32),
            pltpu.VMEM((NZ, 24, 256), f32),
            pltpu.VMEM((NZ, 24, 256), f32),
            pltpu.VMEM((NZ, 24, 256), bf16),
            pltpu.VMEM((NZ - 1, 24, 256), bf16),
            pltpu.VMEM((NY, 24, 256), f32),
            dma(()), dma((NZ - 1,)), dma((NZ - 1,)), dma((8,)), dma((8,)), dma(()),
            dma((8, 8)), dma((8, 8)), dma((8,)), dma((7,)), dma((7,)),
            dma((NX - 1,)), dma((NX - 1,)), dma((NX - 1,)), dma((NX - 1,)), dma(()), dma(()),
            dma((NZ - 1,)), dma((NZ - 1,)), dma((NY - 1,)), dma((NY - 1,)),
            dma((NZ - 1,)), dma((NZ - 1,)), dma(()), dma(()),
        ],
        compiler_params=pltpu.CompilerParams(
            collective_id=1, has_side_effects=True, vmem_limit_bytes=60 * 1024 * 1024
        ),
        name="step",
    )(features, jnp.transpose(owner_of, (1, 2, 0)), jnp.transpose(row_of), w_self, w_neighbor, cotangent)
    return pl.pallas_call(
        finish_kernel,
        out_shape=(
            jax.ShapeDtypeStruct((128, 256), bf16),
            jax.ShapeDtypeStruct((192, 256), f32),
            jax.ShapeDtypeStruct((192, 256), f32),
        ),
        in_specs=[vmem, vmem],
        out_specs=(vmem, vmem, vmem),
        name="finish",
    )(hidden, final)


def solution(mesh):
    return jax.shard_map(
        on_device,
        mesh=mesh,
        in_specs=(
            P("narrow", "wide"),
            P("wide", None, None),
            P("wide", None),
            P("narrow", None),
            P("narrow", None),
            P(("wide", "narrow"), None),
        ),
        out_specs=(P(("wide", "narrow"), None), P("narrow", None), P("narrow", None)),
        check_vma=False,
    )
```

```python
import jax
import jax.numpy as jnp
from jax import lax
from jax.experimental import pallas as pl
from jax.experimental.pallas import tpu as pltpu
from jax.sharding import PartitionSpec as P

FANOUT = 15
NX, NY, NZ = 4, 4, 8
ROOT, CUBE = 0.7978845608, 0.044715


def remote(src, dst, send, recv, target):
    return pltpu.make_async_remote_copy(
        src_ref=src,
        dst_ref=dst,
        send_sem=send,
        recv_sem=recv,
        device_id=target,
        device_id_type=pl.DeviceIdType.MESH,
    )


def place():
    wide = lax.axis_index("wide")
    return wide // 16, lax.rem(wide // 2, 8), lax.rem(wide, 2), lax.axis_index("narrow")


def wide_at(y, z, core):
    return (y * 8 + z) * 2 + core


def order_of(step):
    odd = lax.rem(step, 2)
    return jnp.where(step == 0, 4, jnp.where(odd == 1, 3 - step // 2, 4 + step // 2))


def list_requests(own_ref, row_ref, listed, stacked, spots):
    upper = (
        lax.broadcasted_iota(jnp.int32, (512, 512), 0) < lax.broadcasted_iota(jnp.int32, (512, 512), 1)
    ).astype(jnp.float32).astype(jnp.bfloat16)
    owner_id = lax.broadcasted_iota(jnp.int32, (64, 512), 0)
    slot_id = lax.broadcasted_iota(jnp.int32, (256, 512), 0)
    slot_id = jnp.where(slot_id < 192, slot_id, slot_id - 64)
    lane = lax.broadcasted_iota(jnp.int32, (1, 512), 1)

    def one(j, used):
        owner = own_ref[j]
        row = row_ref[pl.ds(j, 1), :]
        place_of = ((owner >> 1) & 7) * 8 + (owner >> 4) * 2 + (owner & 1)
        mine = owner_id == place_of
        onehot = jnp.where(mine, 1.0, 0.0)
        within = jnp.dot(onehot.astype(jnp.bfloat16), upper, preferred_element_type=jnp.float32)
        slot = jnp.sum(onehot * (within + used), axis=0, keepdims=True).astype(jnp.int32)
        span = pl.ds(pl.multiple_of(j * 512, 512), 512)
        spots[:, span] = jnp.where(slot_id == slot, 1.0, 0.0).astype(jnp.bfloat16)
        for i, piece in enumerate([row & 255, row >> 8, lane & 255, (lane >> 8) + 2 * j + 1]):
            stacked[i * 64:(i + 1) * 64, span] = jnp.where(mine, piece.astype(jnp.float32), 0.0).astype(jnp.bfloat16)
        return used + jnp.sum(onehot, axis=1, keepdims=True)

    lax.fori_loop(0, 16, one, jnp.zeros((64, 1), jnp.float32))
    found = lax.dot_general(
        stacked[...], spots[...], (((1,), (1,)), ((), ())), preferred_element_type=jnp.float32
    )
    found = found.astype(jnp.int32)
    row = found[0:64] + 256 * found[64:128]
    block = found[192:256]
    item = found[128:192] + 256 * (block - 1)
    target = jnp.where(block > 0, jnp.where(item < 512, item, 512 + (item & 511)), 1024)
    listed[...] = (row + 8192 * target).reshape(8, 8, 256)


def step_kernel(
    feat_ref, own_ref, row_ref, ws_ref, wn_ref, cot_ref, hid_ref, final,
    feat, stacked, spots, listed, via, turned, asked, rows_of, index, dest, table, near, outgoing, landed, choose, held, dense, ring, ringed,
    rows, part, part_out, got_part, slopes, grads, got_core, full, full_out, got_z, got_y,
    e_sem, a_send, a_recv, b_send, b_recv, i_sem, f_send, f_recv, o_sem, r_send, r_recv,
    x_send, x_recv, s_send, s_recv, c_send, c_recv, z_send, z_recv, y_send, y_recv, g_send, g_recv, d_send, d_recv,
):
    y, z, core, x = place()
    near_z = [{"wide": wide_at(y, lax.rem(z + k, NZ), core), "narrow": x} for k in range(1, NZ)]
    near_x = [{"wide": wide_at(y, z, core), "narrow": lax.rem(x + k, NX)} for k in range(1, NX)]

    def plane(q):
        return lax.rem(y + q // 2, NY), lax.rem(core + q, 2)

    def plane_at(q):
        there, seat = plane(q)
        return {"wide": wide_at(there, z, seat), "narrow": x}

    barrier = pltpu.get_barrier_semaphore()
    targets = near_z + [plane_at(q) for q in range(1, 8)] + near_x
    for target in targets:
        pl.semaphore_signal(barrier, inc=1, device_id=target, device_id_type=pl.DeviceIdType.MESH)
    feat_copy = pltpu.make_async_copy(feat_ref, feat, e_sem)
    feat_copy.start()
    me = y * 2 + core

    list_requests(own_ref, row_ref, listed, stacked, spots)
    pl.semaphore_wait(barrier, len(targets))
    for k in range(1, NZ):
        remote(listed.at[lax.rem(z + k, NZ)], via.at[z], a_send.at[k - 1], a_recv.at[k - 1], near_z[k - 1]).start()
    via[z] = listed[z]

    eye = (
        lax.broadcasted_iota(jnp.int32, (256, 256), 0) == lax.broadcasted_iota(jnp.int32, (256, 256), 1)
    ).astype(jnp.float32).astype(jnp.bfloat16)

    def turn(b, _):
        start = pl.multiple_of(b * 256, 256)
        block = feat[:, pl.ds(start, 256)]
        block = jnp.concatenate([block, block[128:]], axis=0)
        turned_block = lax.dot_general(eye, block, (((1,), (1,)), ((), ())), preferred_element_type=jnp.float32)
        table[pl.ds(2 * start, 256, stride=2), :] = turned_block[:, :128]
        table[pl.ds(2 * start + 1, 256, stride=2), :] = turned_block[:, 128:]
        return 0

    feat_copy.wait()
    lax.fori_loop(0, 16, turn, 0)
    for k in range(1, NZ):
        remote(listed.at[z], via.at[lax.rem(z + NZ - k, NZ)], a_send.at[k - 1], a_recv.at[k - 1], near_z[k - 1]).wait_recv()
    for group in range(8):
        for owner in range(8):
            turned[owner, group:group + 1] = via[group, owner:owner + 1]

    def tell(q, _):
        there, seat = plane(q)
        remote(turned.at[there * 2 + seat], asked.at[me], b_send.at[q], b_recv.at[q], plane_at(q)).start()
        return 0

    lax.fori_loop(1, 8, tell, 0)
    asked[me] = turned[me]
    for owner in range(8):
        dest[:, owner * 192:(owner + 1) * 192] = turned[owner][:, :192] >> 13
    lax.fori_loop(16, 32, turn, 0)

    def told(q, _):
        remote(turned.at[0], asked.at[0], b_send.at[q], b_recv.at[q], plane_at(q)).wait_recv()
        return 0

    lax.fori_loop(1, 8, told, 0)
    rows_of[...] = 2 * (asked[...] & 8191).reshape(64, 256)
    copy = pltpu.make_async_copy(rows_of, index, i_sem)
    copy.start()
    copy.wait()

    low_half = lax.broadcasted_iota(jnp.int32, (96, 128), 1) < 64
    low_lane = lax.broadcasted_iota(jnp.int32, (512, 128), 1) < 64

    def fetch(step):
        group = lax.rem(z + order_of(step), NZ)

        def one(q, _):
            there, seat = plane(q)
            line = (there * 2 + seat) * 8 + group

            for s in range(192):
                near[2 * s:2 * s + 2, :] = table[pl.ds(index[line, s], 2), :]
            outgoing[step, q, 0:192] = near[pl.ds(0, 192, stride=2), :].astype(jnp.bfloat16)
            outgoing[step, q, 192:288] = jnp.where(
                low_half, near[pl.ds(1, 96, stride=2), :], near[pl.ds(193, 96, stride=2), :]
            ).astype(jnp.bfloat16)

            @pl.when(q > 0)
            def _():
                remote(outgoing.at[step, q], landed.at[step, me], f_send.at[step, q], f_recv.at[step, q], plane_at(q)).start()

            @pl.when(q == 0)
            def _():
                pltpu.make_async_copy(outgoing.at[step, q], landed.at[step, me], o_sem.at[step]).start()

            return 0

        lax.fori_loop(0, 8, one, 0)

    def gather_in(step):
        group = lax.rem(z + order_of(step), NZ)
        target_id = lax.broadcasted_iota(jnp.int32, (1024, 256), 0)
        for b in range(6):
            choose[:, b * 256:(b + 1) * 256] = jnp.where(
                target_id == dest[pl.ds(group, 1), b * 256:(b + 1) * 256], 1.0, 0.0
            ).astype(jnp.bfloat16)
        pltpu.make_async_copy(outgoing.at[step, 0], landed.at[step, me], o_sem.at[step]).wait()

        def got(q, _):
            remote(outgoing.at[step, q], landed.at[step, me], f_send.at[step, q], f_recv.at[step, q], plane_at(q)).wait_recv()
            return 0

        lax.fori_loop(1, 8, got, 0)
        for owner in range(8):
            base = owner * 192
            held[base:base + 192, 0:128] = landed[step, owner, 0:192]
            pair = landed[step, owner, 192:288]
            held[base:base + 96, 128:256] = pair
            held[base + 96:base + 192, 128:256] = pltpu.roll(pair.astype(jnp.float32), 64, 1).astype(jnp.bfloat16)
        for part in range(4):
            dense[part * 256:(part + 1) * 256] = jnp.dot(
                choose[part * 256:(part + 1) * 256], held[...], preferred_element_type=jnp.float32
            )

    def pieces():
        mixed = jnp.where(low_lane, dense[0:512, 128:256], pltpu.roll(dense[512:1024, 128:256], 64, 1))
        return [dense[0:512, 0:128], mixed, dense[512:1024, 0:128]]

    def ring_at(step):
        up = jnp.logical_or(step == 0, lax.rem(step, 2) == 1)
        return {"wide": wide_at(y, lax.rem(z + jnp.where(up, 1, NZ - 1), NZ), core), "narrow": x}

    def ring_copy(step):
        return remote(ring.at[step], ringed.at[step], r_send.at[step], r_recv.at[step], ring_at(step))

    def pass_on(step):
        @pl.when(jnp.logical_or(step == 0, step == 2))
        def _():
            for i, piece in enumerate(pieces()):
                ring[step, i] = piece.astype(jnp.bfloat16)

        @pl.when(jnp.logical_and(step != 0, step != 2))
        def _():
            before = jnp.where(step == 1, 0, step - 2)
            ring_copy(before).wait_recv()
            for i, piece in enumerate(pieces()):
                ring[step, i] = (piece + ringed[before, i].astype(jnp.float32)).astype(jnp.bfloat16)

        ring_copy(step).start()

    def early(step, _):
        fetch(step)
        return 0

    lax.fori_loop(0, 3, early, 0)

    def loop(step, _):
        @pl.when(step < 5)
        def _():
            fetch(step + 3)

        gather_in(step)
        pass_on(step)
        return 0

    lax.fori_loop(0, 7, loop, 0)
    gather_in(7)
    ring_copy(5).wait_recv()
    ring_copy(6).wait_recv()
    for i, piece in enumerate(pieces()):
        total = piece + ringed[5, i].astype(jnp.float32) + ringed[6, i].astype(jnp.float32)
        if i == 1:
            total = jnp.where(low_lane, total, total / FANOUT)
        if i == 2:
            total = total / FANOUT
        rows[:, i * 128:(i + 1) * 128] = total.astype(jnp.bfloat16)

    middle = jnp.concatenate([ws_ref[128:192], wn_ref[128:192]], axis=0)
    for k in range(NX):
        span = slice(k * 128, (k + 1) * 128)
        value = jnp.dot(rows[span, 0:128], ws_ref[0:128], preferred_element_type=jnp.float32)
        value = value + jnp.dot(rows[span, 128:256], middle, preferred_element_type=jnp.float32)
        value = value + jnp.dot(rows[span, 256:384], wn_ref[0:128], preferred_element_type=jnp.float32)
        part[k] = value
        part_out[k] = value.astype(jnp.bfloat16)
    sent = []
    for k in range(1, NX):
        copy = remote(part_out.at[lax.rem(x + k, NX)], got_part.at[k - 1], x_send.at[k - 1], x_recv.at[k - 1], near_x[k - 1])
        copy.start()
        sent.append(copy)
    value = part[x]
    for k in range(1, NX):
        sent[k - 1].wait_recv()
        value = value + got_part[k - 1].astype(jnp.float32)
    bend = jnp.tanh(ROOT * (value + CUBE * value * value * value))
    rise = 0.5 * (1.0 + bend) + 0.5 * value * (1.0 - bend * bend) * ROOT * (1.0 + 3.0 * CUBE * value * value)
    slopes[x] = (cot_ref[...].astype(jnp.float32) * rise).astype(jnp.bfloat16)
    for k in range(1, NX):
        copy = remote(slopes.at[x], slopes.at[x], s_send.at[k - 1], s_recv.at[k - 1], near_x[k - 1])
        copy.start()
        sent.append(copy)
    hid_ref[...] = (0.5 * value * (1.0 + bend)).astype(jnp.bfloat16)
    for k in range(1, NX):
        remote(slopes.at[x], slopes.at[lax.rem(x + NX - k, NX)], s_send.at[k - 1], s_recv.at[k - 1], near_x[k - 1]).wait_recv()
    grads[...] = lax.dot_general(
        rows[...], slopes[...].reshape(512, 256), (((0,), (0,)), ((), ())), preferred_element_type=jnp.float32
    ).reshape(2, NZ, 24, 256)
    copy = remote(grads.at[1 - core], got_core, c_send, c_recv, plane_at(1))
    copy.start()
    sent.append(copy)
    copy.wait_recv()
    full[...] = grads[core] + got_core[...]
    full_out[...] = full[...].astype(jnp.bfloat16)
    for k in range(1, NZ):
        copy = remote(full_out.at[lax.rem(z + k, NZ)], got_z.at[k - 1], z_send.at[k - 1], z_recv.at[k - 1], near_z[k - 1])
        copy.start()
        sent.append(copy)
    mine = full[z]
    for k in range(1, NZ):
        remote(full_out.at[z], got_z.at[k - 1], z_send.at[k - 1], z_recv.at[k - 1], near_z[k - 1]).wait_recv()
        mine = mine + got_z[k - 1].astype(jnp.float32)
    got_y[y] = mine
    for k in range(1, NY):
        copy = remote(got_y.at[y], got_y.at[y], y_send.at[k - 1], y_recv.at[k - 1], plane_at(2 * k))
        copy.start()
        sent.append(copy)
    for k in range(1, NY):
        remote(got_y.at[y], got_y.at[lax.rem(y + NY - k, NY)], y_send.at[k - 1], y_recv.at[k - 1], plane_at(2 * k)).wait_recv()
    final[core, z] = (got_y[0] + got_y[1] + got_y[2] + got_y[3]).astype(jnp.bfloat16)
    for k in range(1, NZ):
        copy = remote(final.at[core, z], final.at[core, z], g_send.at[k - 1], g_recv.at[k - 1], near_z[k - 1])
        copy.start()
        sent.append(copy)
    for k in range(1, NZ):
        remote(final.at[core, z], final.at[core, lax.rem(z + NZ - k, NZ)], g_send.at[k - 1], g_recv.at[k - 1], near_z[k - 1]).wait_recv()
    copy = remote(final.at[core], final.at[core], d_send, d_recv, plane_at(1))
    copy.start()
    sent.append(copy)
    remote(final.at[core], final.at[1 - core], d_send, d_recv, plane_at(1)).wait_recv()
    for copy in sent:
        copy.wait_send()

    for k in range(1, NZ):
        remote(listed.at[z], via.at[z], a_send.at[k - 1], a_recv.at[k - 1], near_z[k - 1]).wait_send()

    def drain(q, _):
        remote(turned.at[0], asked.at[0], b_send.at[q], b_recv.at[q], plane_at(q)).wait_send()

        def each(step, _):
            remote(outgoing.at[step, q], landed.at[step, me], f_send.at[step, q], f_recv.at[step, q], plane_at(q)).wait_send()
            return 0

        lax.fori_loop(0, 8, each, 0)
        return 0

    lax.fori_loop(1, 8, drain, 0)

    def drain_ring(step, _):
        ring_copy(step).wait_send()
        return 0

    lax.fori_loop(0, 7, drain_ring, 0)


def finish_kernel(hid_ref, final_ref, out_ref, gs_ref, gn_ref):
    out_ref[...] = hid_ref[...]
    whole = final_ref[...].astype(jnp.float32).reshape(384, 256)
    gs_ref[...] = whole[:192]
    gn_ref[0:128] = whole[256:]
    gn_ref[128:192] = whole[192:256]


def on_device(features, owner_of, row_of, w_self, w_neighbor, cotangent):
    vmem = pl.BlockSpec(memory_space=pltpu.VMEM)
    dma = pltpu.SemaphoreType.DMA
    f32, bf16, i32 = jnp.float32, jnp.bfloat16, jnp.int32
    hidden, final = pl.pallas_call(
        step_kernel,
        out_shape=(jax.ShapeDtypeStruct((128, 256), bf16), jax.ShapeDtypeStruct((2, NZ, 24, 256), bf16)),
        in_specs=[pl.BlockSpec(memory_space=pl.ANY)] + [vmem] * 5,
        out_specs=(vmem, vmem),
        scratch_shapes=[
            pltpu.VMEM((192, 8192), bf16),
            pltpu.VMEM((256, 8192), bf16),
            pltpu.VMEM((256, 8192), bf16),
            pltpu.VMEM((8, 8, 256), i32),
            pltpu.VMEM((8, 8, 256), i32),
            pltpu.VMEM((8, 8, 256), i32),
            pltpu.VMEM((8, 8, 256), i32),
            pltpu.VMEM((64, 256), i32),
            pltpu.SMEM((64, 256), i32),
            pltpu.VMEM((8, 1536), i32),
            pltpu.VMEM((16384, 128), f32),
            pltpu.VMEM((384, 128), f32),
            pltpu.VMEM((8, 8, 288, 128), bf16),
            pltpu.VMEM((8, 8, 288, 128), bf16),
            pltpu.VMEM((1024, 1536), bf16),
            pltpu.VMEM((1536, 256), bf16),
            pltpu.VMEM((1024, 256), f32),
            pltpu.VMEM((7, 3, 512, 128), bf16),
            pltpu.VMEM((7, 3, 512, 128), bf16),
            pltpu.VMEM((512, 384), bf16),
            pltpu.VMEM((NX, 128, 256), f32),
            pltpu.VMEM((NX, 128, 256), bf16),
            pltpu.VMEM((NX - 1, 128, 256), bf16),
            pltpu.VMEM((NX, 128, 256), bf16),
            pltpu.VMEM((2, NZ, 24, 256), f32),
            pltpu.VMEM((NZ, 24, 256), f32),
            pltpu.VMEM((NZ, 24, 256), f32),
            pltpu.VMEM((NZ, 24, 256), bf16),
            pltpu.VMEM((NZ - 1, 24, 256), bf16),
            pltpu.VMEM((NY, 24, 256), f32),
            dma(()), dma((NZ - 1,)), dma((NZ - 1,)), dma((8,)), dma((8,)), dma(()),
            dma((8, 8)), dma((8, 8)), dma((8,)), dma((7,)), dma((7,)),
            dma((NX - 1,)), dma((NX - 1,)), dma((NX - 1,)), dma((NX - 1,)), dma(()), dma(()),
            dma((NZ - 1,)), dma((NZ - 1,)), dma((NY - 1,)), dma((NY - 1,)),
            dma((NZ - 1,)), dma((NZ - 1,)), dma(()), dma(()),
        ],
        compiler_params=pltpu.CompilerParams(
            collective_id=1, has_side_effects=True, vmem_limit_bytes=60 * 1024 * 1024
        ),
        name="step",
    )(features, jnp.transpose(owner_of, (1, 2, 0)), jnp.transpose(row_of), w_self, w_neighbor, cotangent)
    return pl.pallas_call(
        finish_kernel,
        out_shape=(
            jax.ShapeDtypeStruct((128, 256), bf16),
            jax.ShapeDtypeStruct((192, 256), f32),
            jax.ShapeDtypeStruct((192, 256), f32),
        ),
        in_specs=[vmem, vmem],
        out_specs=(vmem, vmem, vmem),
        name="finish",
    )(hidden, final)


def solution(mesh):
    return jax.shard_map(
        on_device,
        mesh=mesh,
        in_specs=(
            P("narrow", "wide"),
            P("wide", None, None),
            P("wide", None),
            P("narrow", None),
            P("narrow", None),
            P(("wide", "narrow"), None),
        ),
        out_specs=(P(("wide", "narrow"), None), P("narrow", None), P("narrow", None)),
        check_vma=False,
    )
```

```python
import jax
import jax.numpy as jnp
from jax import lax
from jax.experimental import pallas as pl
from jax.experimental.pallas import tpu as pltpu
from jax.sharding import PartitionSpec as P

FANOUT = 15
NX, NY, NZ = 4, 4, 8
ROOT, CUBE = 0.7978845608, 0.044715


def remote(src, dst, send, recv, target):
    return pltpu.make_async_remote_copy(
        src_ref=src,
        dst_ref=dst,
        send_sem=send,
        recv_sem=recv,
        device_id=target,
        device_id_type=pl.DeviceIdType.MESH,
    )


def place():
    wide = lax.axis_index("wide")
    return wide // 16, lax.rem(wide // 2, 8), lax.rem(wide, 2), lax.axis_index("narrow")


def wide_at(y, z, core):
    return (y * 8 + z) * 2 + core


def order_of(step):
    odd = lax.rem(step, 2)
    return jnp.where(step == 0, 4, jnp.where(odd == 1, 3 - step // 2, 4 + step // 2))


def list_requests(own_ref, row_ref, listed, stacked, spots):
    upper = (
        lax.broadcasted_iota(jnp.int32, (512, 512), 0) < lax.broadcasted_iota(jnp.int32, (512, 512), 1)
    ).astype(jnp.float32).astype(jnp.bfloat16)
    owner_id = lax.broadcasted_iota(jnp.int32, (64, 512), 0)
    slot_id = lax.broadcasted_iota(jnp.int32, (256, 512), 0)
    slot_id = jnp.where(slot_id < 192, slot_id, slot_id - 64)
    lane = lax.broadcasted_iota(jnp.int32, (1, 512), 1)

    def one(j, used):
        owner = own_ref[j]
        row = row_ref[pl.ds(j, 1), :]
        place_of = ((owner >> 1) & 7) * 8 + (owner >> 4) * 2 + (owner & 1)
        mine = owner_id == place_of
        onehot = jnp.where(mine, 1.0, 0.0)
        within = jnp.dot(onehot.astype(jnp.bfloat16), upper, preferred_element_type=jnp.float32)
        slot = jnp.sum(onehot * (within + used), axis=0, keepdims=True).astype(jnp.int32)
        span = pl.ds(pl.multiple_of(j * 512, 512), 512)
        spots[:, span] = jnp.where(slot_id == slot, 1.0, 0.0).astype(jnp.bfloat16)
        for i, piece in enumerate([row & 255, row >> 8, lane & 255, (lane >> 8) + 2 * j + 1]):
            stacked[i * 64:(i + 1) * 64, span] = jnp.where(mine, piece.astype(jnp.float32), 0.0).astype(jnp.bfloat16)
        return used + jnp.sum(onehot, axis=1, keepdims=True)

    lax.fori_loop(0, 16, one, jnp.zeros((64, 1), jnp.float32))
    found = lax.dot_general(
        stacked[...], spots[...], (((1,), (1,)), ((), ())), preferred_element_type=jnp.float32
    )
    found = found.astype(jnp.int32)
    row = found[0:64] + 256 * found[64:128]
    block = found[192:256]
    item = found[128:192] + 256 * (block - 1)
    target = jnp.where(block > 0, jnp.where(item < 512, item, 512 + (item & 511)), 1024)
    listed[...] = (row + 8192 * target).reshape(8, 8, 1, 256)


def step_kernel(
    feat_ref, own_ref, row_ref, ws_ref, wn_ref, cot_ref, hid_ref, final,
    feat, stacked, spots, listed, via, asked, rows_of, index, dest, table, near, outgoing, landed, choose, held, dense, ring, ringed,
    rows, part, part_out, got_part, slopes, flat, grads, got_core, full, full_out, got_z,
    e_sem, a_send, a_recv, b_send, b_recv, i_sem, f_send, f_recv, o_sem, r_send, r_recv,
    x_send, x_recv, s_send, s_recv, c_send, c_recv, z_send, z_recv, g_send, g_recv, d_send, d_recv,
):
    y, z, core, x = place()
    ys = [y] + [lax.rem(y + k, NY) for k in range(1, NY)]
    zs = [z] + [lax.rem(z + k, NZ) for k in range(1, NZ)]
    seats = [core, 1 - core]
    everyone = [(dy, dz, dc) for dy in range(NY) for dz in range(NZ) for dc in range(2) if dy + dz + dc > 0]
    column = [(dy, dz) for dy in range(NY) for dz in range(NZ) if dy + dz > 0]

    def at(dy, dz, dc):
        return {"wide": wide_at(ys[dy], zs[dz], seats[dc]), "narrow": x}

    near_z = [at(0, k, 0) for k in range(1, NZ)]
    near_x = [{"wide": wide_at(y, z, core), "narrow": lax.rem(x + k, NX)} for k in range(1, NX)]

    def plane(q):
        return lax.rem(y + q // 2, NY), lax.rem(core + q, 2)

    def plane_at(q):
        there, seat = plane(q)
        return {"wide": wide_at(there, z, seat), "narrow": x}

    barrier = pltpu.get_barrier_semaphore()
    targets = [at(*peer) for peer in everyone] + near_x
    for target in targets:
        pl.semaphore_signal(barrier, inc=1, device_id=target, device_id_type=pl.DeviceIdType.MESH)
    feat_copy = pltpu.make_async_copy(feat_ref, feat, e_sem)
    feat_copy.start()
    me = y * 2 + core

    list_requests(own_ref, row_ref, listed, stacked, spots)
    pl.semaphore_wait(barrier, len(targets))
    for dy, dz, dc in everyone:
        remote(
            listed.at[zs[dz], ys[dy] * 2 + seats[dc]], asked.at[me, z],
            b_send.at[dy * 16 + dz * 2 + dc], b_recv.at[dy * 16 + dz * 2 + dc], at(dy, dz, dc),
        ).start()
    for k in range(1, NZ):
        remote(listed.at[zs[k]], via.at[z], a_send.at[k - 1], a_recv.at[k - 1], near_z[k - 1]).start()
    asked[me, z] = listed[z, me]
    via[z] = listed[z]

    eye = (
        lax.broadcasted_iota(jnp.int32, (256, 256), 0) == lax.broadcasted_iota(jnp.int32, (256, 256), 1)
    ).astype(jnp.float32).astype(jnp.bfloat16)

    def turn(b, _):
        start = pl.multiple_of(b * 256, 256)
        block = feat[:, pl.ds(start, 256)]
        block = jnp.concatenate([block, block[128:]], axis=0)
        turned_block = lax.dot_general(eye, block, (((1,), (1,)), ((), ())), preferred_element_type=jnp.float32)
        table[pl.ds(2 * start, 256, stride=2), :] = turned_block[:, :128]
        table[pl.ds(2 * start + 1, 256, stride=2), :] = turned_block[:, 128:]
        return 0

    feat_copy.wait()
    lax.fori_loop(0, 32, turn, 0)
    for dy, dz, dc in everyone:
        remote(
            listed.at[z, me], asked.at[me, z],
            b_send.at[dy * 16 + dz * 2 + dc], b_recv.at[dy * 16 + dz * 2 + dc], at(dy, dz, dc),
        ).wait_recv()
    rows_of[...] = 2 * (asked[...] & 8191).reshape(64, 256)
    copy = pltpu.make_async_copy(rows_of, index, i_sem)
    copy.start()
    copy.wait()

    low_half = lax.broadcasted_iota(jnp.int32, (96, 128), 1) < 64
    low_lane = lax.broadcasted_iota(jnp.int32, (512, 128), 1) < 64

    def fetch(step):
        group = lax.rem(z + order_of(step), NZ)

        def one(q, _):
            there, seat = plane(q)
            line = (there * 2 + seat) * 8 + group

            for s in range(192):
                near[2 * s:2 * s + 2, :] = table[pl.ds(index[line, s], 2), :]
            outgoing[step, q, 0:192] = near[pl.ds(0, 192, stride=2), :].astype(jnp.bfloat16)
            outgoing[step, q, 192:288] = jnp.where(
                low_half, near[pl.ds(1, 96, stride=2), :], near[pl.ds(193, 96, stride=2), :]
            ).astype(jnp.bfloat16)

            @pl.when(q > 0)
            def _():
                remote(outgoing.at[step, q], landed.at[step, me], f_send.at[step, q], f_recv.at[step, q], plane_at(q)).start()

            @pl.when(q == 0)
            def _():
                pltpu.make_async_copy(outgoing.at[step, q], landed.at[step, me], o_sem.at[step]).start()

            return 0

        lax.fori_loop(0, 8, one, 0)

    def gather_in(step):
        group = lax.rem(z + order_of(step), NZ)
        target_id = lax.broadcasted_iota(jnp.int32, (1024, 256), 0)
        for b in range(6):
            choose[:, b * 256:(b + 1) * 256] = jnp.where(
                target_id == dest[pl.ds(group, 1), b * 256:(b + 1) * 256], 1.0, 0.0
            ).astype(jnp.bfloat16)
        pltpu.make_async_copy(outgoing.at[step, 0], landed.at[step, me], o_sem.at[step]).wait()

        def got(q, _):
            remote(outgoing.at[step, q], landed.at[step, me], f_send.at[step, q], f_recv.at[step, q], plane_at(q)).wait_recv()
            return 0

        lax.fori_loop(1, 8, got, 0)
        for owner in range(8):
            base = owner * 192
            held[base:base + 192, 0:128] = landed[step, owner, 0:192]
            pair = landed[step, owner, 192:288]
            held[base:base + 96, 128:256] = pair
            held[base + 96:base + 192, 128:256] = pltpu.roll(pair.astype(jnp.float32), 64, 1).astype(jnp.bfloat16)
        for part in range(4):
            dense[part * 256:(part + 1) * 256] = jnp.dot(
                choose[part * 256:(part + 1) * 256], held[...], preferred_element_type=jnp.float32
            )

    def pieces():
        mixed = jnp.where(low_lane, dense[0:512, 128:256], pltpu.roll(dense[512:1024, 128:256], 64, 1))
        return [dense[0:512, 0:128], mixed, dense[512:1024, 0:128]]

    def ring_at(step):
        up = jnp.logical_or(step == 0, lax.rem(step, 2) == 1)
        return {"wide": wide_at(y, lax.rem(z + jnp.where(up, 1, NZ - 1), NZ), core), "narrow": x}

    def ring_copy(step):
        return remote(ring.at[step], ringed.at[step], r_send.at[step], r_recv.at[step], ring_at(step))

    def pass_on(step):
        @pl.when(jnp.logical_or(step == 0, step == 2))
        def _():
            for i, piece in enumerate(pieces()):
                ring[step, i] = piece.astype(jnp.bfloat16)

        @pl.when(jnp.logical_and(step != 0, step != 2))
        def _():
            before = jnp.where(step == 1, 0, step - 2)
            ring_copy(before).wait_recv()
            for i, piece in enumerate(pieces()):
                ring[step, i] = (piece + ringed[before, i].astype(jnp.float32)).astype(jnp.bfloat16)

        ring_copy(step).start()

    def early(step, _):
        fetch(step)
        return 0

    lax.fori_loop(0, 3, early, 0)
    for k in range(1, NZ):
        remote(listed.at[z], via.at[lax.rem(z + NZ - k, NZ)], a_send.at[k - 1], a_recv.at[k - 1], near_z[k - 1]).wait_recv()
    for owner in range(8):
        dest[:, owner * 192:(owner + 1) * 192] = via[:, owner].reshape(8, 256)[:, :192] >> 13

    def loop(step, _):
        @pl.when(step < 5)
        def _():
            fetch(step + 3)

        gather_in(step)
        pass_on(step)
        return 0

    lax.fori_loop(0, 7, loop, 0)
    gather_in(7)
    ring_copy(5).wait_recv()
    ring_copy(6).wait_recv()
    for i, piece in enumerate(pieces()):
        total = piece + ringed[5, i].astype(jnp.float32) + ringed[6, i].astype(jnp.float32)
        if i == 1:
            total = jnp.where(low_lane, total, total / FANOUT)
        if i == 2:
            total = total / FANOUT
        rows[:, i * 128:(i + 1) * 128] = total.astype(jnp.bfloat16)

    middle = jnp.concatenate([ws_ref[128:192], wn_ref[128:192]], axis=0)
    for k in range(NX):
        span = slice(k * 128, (k + 1) * 128)
        value = jnp.dot(rows[span, 0:128], ws_ref[0:128], preferred_element_type=jnp.float32)
        value = value + jnp.dot(rows[span, 128:256], middle, preferred_element_type=jnp.float32)
        value = value + jnp.dot(rows[span, 256:384], wn_ref[0:128], preferred_element_type=jnp.float32)
        part[k] = value
        part_out[k] = value.astype(jnp.bfloat16)
    sent = []
    for k in range(1, NX):
        copy = remote(part_out.at[lax.rem(x + k, NX)], got_part.at[k - 1], x_send.at[k - 1], x_recv.at[k - 1], near_x[k - 1])
        copy.start()
        sent.append(copy)
    value = part[x]
    for k in range(1, NX):
        sent[k - 1].wait_recv()
        value = value + got_part[k - 1].astype(jnp.float32)
    bend = jnp.tanh(ROOT * (value + CUBE * value * value * value))
    rise = 0.5 * (1.0 + bend) + 0.5 * value * (1.0 - bend * bend) * ROOT * (1.0 + 3.0 * CUBE * value * value)
    slopes[x] = (cot_ref[...].astype(jnp.float32) * rise).astype(jnp.bfloat16)
    for k in range(1, NX):
        copy = remote(slopes.at[x], slopes.at[x], s_send.at[k - 1], s_recv.at[k - 1], near_x[k - 1])
        copy.start()
        sent.append(copy)
    hid_ref[...] = (0.5 * value * (1.0 + bend)).astype(jnp.bfloat16)
    for k in range(1, NX):
        remote(slopes.at[x], slopes.at[lax.rem(x + NX - k, NX)], s_send.at[k - 1], s_recv.at[k - 1], near_x[k - 1]).wait_recv()
    flat[...] = lax.dot_general(
        rows[...], slopes[...].reshape(512, 256), (((0,), (0,)), ((), ())), preferred_element_type=jnp.float32
    )
    for half in range(2):
        for piece in range(32):
            grads[half, piece] = flat[half * 192 + piece * 6:half * 192 + piece * 6 + 6]
    copy = remote(grads.at[1 - core], got_core, c_send, c_recv, plane_at(1))
    copy.start()
    sent.append(copy)
    copy.wait_recv()
    full[...] = grads[core] + got_core[...]
    full_out[...] = full[...].astype(jnp.bfloat16)
    spot = y * NZ + z
    for dy, dz in column:
        copy = remote(
            full_out.at[ys[dy] * NZ + zs[dz]], got_z.at[dy * NZ + dz],
            z_send.at[dy * NZ + dz], z_recv.at[dy * NZ + dz], at(dy, dz, 0),
        )
        copy.start()
        sent.append(copy)
    mine = full[spot]
    for dy, dz in column:
        remote(
            full_out.at[spot], got_z.at[dy * NZ + dz], z_send.at[dy * NZ + dz], z_recv.at[dy * NZ + dz], at(dy, dz, 0)
        ).wait_recv()
        mine = mine + got_z[dy * NZ + dz].astype(jnp.float32)
    final[core, spot] = mine.astype(jnp.bfloat16)
    for dy, dz in column:
        copy = remote(
            final.at[core, spot], final.at[core, spot], g_send.at[dy * NZ + dz], g_recv.at[dy * NZ + dz], at(dy, dz, 0)
        )
        copy.start()
        sent.append(copy)
    for dy, dz in column:
        there = ys[(NY - dy) % NY] * NZ + zs[(NZ - dz) % NZ]
        remote(
            final.at[core, spot], final.at[core, there], g_send.at[dy * NZ + dz], g_recv.at[dy * NZ + dz], at(dy, dz, 0)
        ).wait_recv()
    copy = remote(final.at[core], final.at[core], d_send, d_recv, plane_at(1))
    copy.start()
    sent.append(copy)
    remote(final.at[core], final.at[1 - core], d_send, d_recv, plane_at(1)).wait_recv()
    for copy in sent:
        copy.wait_send()

    for k in range(1, NZ):
        remote(listed.at[z], via.at[z], a_send.at[k - 1], a_recv.at[k - 1], near_z[k - 1]).wait_send()

    for dy, dz, dc in everyone:
        remote(
            listed.at[z, me], asked.at[me, z],
            b_send.at[dy * 16 + dz * 2 + dc], b_recv.at[dy * 16 + dz * 2 + dc], at(dy, dz, dc),
        ).wait_send()

    def drain(q, _):
        def each(step, _):
            remote(outgoing.at[step, q], landed.at[step, me], f_send.at[step, q], f_recv.at[step, q], plane_at(q)).wait_send()
            return 0

        lax.fori_loop(0, 8, each, 0)
        return 0

    lax.fori_loop(1, 8, drain, 0)

    def drain_ring(step, _):
        ring_copy(step).wait_send()
        return 0

    lax.fori_loop(0, 7, drain_ring, 0)


def finish_kernel(hid_ref, final_ref, out_ref, gs_ref, gn_ref):
    out_ref[...] = hid_ref[...]
    for piece in range(32):
        first = piece * 6
        gs_ref[first:first + 6] = final_ref[0, piece].astype(jnp.float32)
        block = final_ref[1, piece].astype(jnp.float32)
        low = min(6, max(0, 64 - first))
        if low > 0:
            gn_ref[128 + first:128 + first + low] = block[:low]
        if low < 6:
            gn_ref[first + low - 64:first - 58] = block[low:]


def on_device(features, owner_of, row_of, w_self, w_neighbor, cotangent):
    vmem = pl.BlockSpec(memory_space=pltpu.VMEM)
    dma = pltpu.SemaphoreType.DMA
    f32, bf16, i32 = jnp.float32, jnp.bfloat16, jnp.int32
    hidden, final = pl.pallas_call(
        step_kernel,
        out_shape=(jax.ShapeDtypeStruct((128, 256), bf16), jax.ShapeDtypeStruct((2, 32, 6, 256), bf16)),
        in_specs=[pl.BlockSpec(memory_space=pl.ANY)] + [vmem] * 5,
        out_specs=(vmem, vmem),
        scratch_shapes=[
            pltpu.VMEM((192, 8192), bf16),
            pltpu.VMEM((256, 8192), bf16),
            pltpu.VMEM((256, 8192), bf16),
            pltpu.VMEM((8, 8, 1, 256), i32),
            pltpu.VMEM((8, 8, 1, 256), i32),
            pltpu.VMEM((8, 8, 1, 256), i32),
            pltpu.VMEM((64, 256), i32),
            pltpu.SMEM((64, 256), i32),
            pltpu.VMEM((8, 1536), i32),
            pltpu.VMEM((16384, 128), f32),
            pltpu.VMEM((384, 128), f32),
            pltpu.VMEM((8, 8, 288, 128), bf16),
            pltpu.VMEM((8, 8, 288, 128), bf16),
            pltpu.VMEM((1024, 1536), bf16),
            pltpu.VMEM((1536, 256), bf16),
            pltpu.VMEM((1024, 256), f32),
            pltpu.VMEM((7, 3, 512, 128), bf16),
            pltpu.VMEM((7, 3, 512, 128), bf16),
            pltpu.VMEM((512, 384), bf16),
            pltpu.VMEM((NX, 128, 256), f32),
            pltpu.VMEM((NX, 128, 256), bf16),
            pltpu.VMEM((NX - 1, 128, 256), bf16),
            pltpu.VMEM((NX, 128, 256), bf16),
            pltpu.VMEM((384, 256), f32),
            pltpu.VMEM((2, 32, 6, 256), f32),
            pltpu.VMEM((32, 6, 256), f32),
            pltpu.VMEM((32, 6, 256), f32),
            pltpu.VMEM((32, 6, 256), bf16),
            pltpu.VMEM((32, 6, 256), bf16),
            dma(()), dma((NZ - 1,)), dma((NZ - 1,)), dma((64,)), dma((64,)), dma(()),
            dma((8, 8)), dma((8, 8)), dma((8,)), dma((7,)), dma((7,)),
            dma((NX - 1,)), dma((NX - 1,)), dma((NX - 1,)), dma((NX - 1,)), dma(()), dma(()),
            dma((32,)), dma((32,)), dma((32,)), dma((32,)), dma(()), dma(()),
        ],
        compiler_params=pltpu.CompilerParams(
            collective_id=1, has_side_effects=True, vmem_limit_bytes=60 * 1024 * 1024
        ),
        name="step",
    )(features, jnp.transpose(owner_of, (1, 2, 0)), jnp.transpose(row_of), w_self, w_neighbor, cotangent)
    return pl.pallas_call(
        finish_kernel,
        out_shape=(
            jax.ShapeDtypeStruct((128, 256), bf16),
            jax.ShapeDtypeStruct((192, 256), f32),
            jax.ShapeDtypeStruct((192, 256), f32),
        ),
        in_specs=[vmem, vmem],
        out_specs=(vmem, vmem, vmem),
        name="finish",
    )(hidden, final)


def solution(mesh):
    return jax.shard_map(
        on_device,
        mesh=mesh,
        in_specs=(
            P("narrow", "wide"),
            P("wide", None, None),
            P("wide", None),
            P("narrow", None),
            P("narrow", None),
            P(("wide", "narrow"), None),
        ),
        out_specs=(P(("wide", "narrow"), None), P("narrow", None), P("narrow", None)),
        check_vma=False,
    )
```

```python
import jax
import jax.numpy as jnp
from jax import lax
from jax.experimental import pallas as pl
from jax.experimental.pallas import tpu as pltpu
from jax.sharding import PartitionSpec as P

FANOUT = 15
NX, NY, NZ = 4, 4, 8
ROOT, CUBE = 0.7978845608, 0.044715


def remote(src, dst, send, recv, target):
    return pltpu.make_async_remote_copy(
        src_ref=src,
        dst_ref=dst,
        send_sem=send,
        recv_sem=recv,
        device_id=target,
        device_id_type=pl.DeviceIdType.MESH,
    )


def place():
    wide = lax.axis_index("wide")
    return wide // 16, lax.rem(wide // 2, 8), lax.rem(wide, 2), lax.axis_index("narrow")


def wide_at(y, z, core):
    return (y * 8 + z) * 2 + core


def order_of(step):
    odd = lax.rem(step, 2)
    return jnp.where(step == 0, 4, jnp.where(odd == 1, 3 - step // 2, 4 + step // 2))


def list_requests(own_ref, row_ref, listed, stacked, spots):
    upper = (
        lax.broadcasted_iota(jnp.int32, (512, 512), 0) < lax.broadcasted_iota(jnp.int32, (512, 512), 1)
    ).astype(jnp.float32).astype(jnp.bfloat16)
    owner_id = lax.broadcasted_iota(jnp.int32, (64, 512), 0)
    slot_id = lax.broadcasted_iota(jnp.int32, (192, 512), 0)
    lane = lax.broadcasted_iota(jnp.int32, (1, 512), 1)

    def one(j, used):
        owner = own_ref[j]
        row = row_ref[pl.ds(j, 1), :]
        place_of = ((owner >> 1) & 7) * 8 + (owner >> 4) * 2 + (owner & 1)
        mine = owner_id == place_of
        onehot = jnp.where(mine, 1.0, 0.0)
        short = onehot.astype(jnp.bfloat16)
        within = jnp.dot(short, upper, preferred_element_type=jnp.float32)
        slot = jnp.sum(onehot * (within + used), axis=0, keepdims=True).astype(jnp.int32)
        span = pl.ds(pl.multiple_of(j * 512, 512), 512)
        spots[:, span] = jnp.where(slot_id == slot, 1.0, 0.0).astype(jnp.bfloat16)
        for i, piece in enumerate([row & 255, row >> 8, lane & 255, (lane >> 8) + 2 * j + 1]):
            stacked[i * 64:(i + 1) * 64, span] = short * piece.astype(jnp.float32).astype(jnp.bfloat16)
        return used + jnp.sum(onehot, axis=1, keepdims=True)

    lax.fori_loop(0, 16, one, jnp.zeros((64, 1), jnp.float32))
    found = lax.dot_general(
        stacked[...], spots[...], (((1,), (1,)), ((), ())), preferred_element_type=jnp.float32
    )
    found = found.astype(jnp.int32)
    row = found[0:64] + 256 * found[64:128]
    block = found[192:256]
    item = found[128:192] + 256 * (block - 1)
    target = jnp.where(block > 0, jnp.where(item < 512, item, 512 + (item & 511)), 1024)
    listed[...] = jnp.zeros_like(listed)
    listed[:, :, 0:192] = (row + 8192 * target).reshape(8, 8, 192)


def step_kernel(
    feat_ref, own_ref, row_ref, ws_ref, wn_ref, cot_ref, hid_ref, final,
    feat, stacked, spots, listed, via, turned, asked, rows_of, index, dest, table, near, outgoing, landed, choose, held, dense, ring, ringed,
    rows, part, part_out, got_part, slopes, grads, got_core, full, full_out, got_z, got_y,
    e_sem, a_send, a_recv, b_send, b_recv, i_sem, f_send, f_recv, o_sem, r_send, r_recv,
    x_send, x_recv, s_send, s_recv, c_send, c_recv, z_send, z_recv, y_send, y_recv, g_send, g_recv, d_send, d_recv,
):
    y, z, core, x = place()
    near_z = [{"wide": wide_at(y, lax.rem(z + k, NZ), core), "narrow": x} for k in range(1, NZ)]
    near_x = [{"wide": wide_at(y, z, core), "narrow": lax.rem(x + k, NX)} for k in range(1, NX)]

    def plane(q):
        return lax.rem(y + q // 2, NY), lax.rem(core + q, 2)

    def plane_at(q):
        there, seat = plane(q)
        return {"wide": wide_at(there, z, seat), "narrow": x}

    barrier = pltpu.get_barrier_semaphore()
    targets = near_z + [plane_at(q) for q in range(1, 8)] + near_x
    for target in targets:
        pl.semaphore_signal(barrier, inc=1, device_id=target, device_id_type=pl.DeviceIdType.MESH)
    feat_copy = pltpu.make_async_copy(feat_ref, feat, e_sem)
    feat_copy.start()
    me = y * 2 + core

    list_requests(own_ref, row_ref, listed, stacked, spots)
    pl.semaphore_wait(barrier, len(targets))
    for k in range(1, NZ):
        remote(listed.at[lax.rem(z + k, NZ)], via.at[z], a_send.at[k - 1], a_recv.at[k - 1], near_z[k - 1]).start()
    via[z] = listed[z]

    eye = (
        lax.broadcasted_iota(jnp.int32, (256, 256), 0) == lax.broadcasted_iota(jnp.int32, (256, 256), 1)
    ).astype(jnp.float32).astype(jnp.bfloat16)

    def turn(b, _):
        start = pl.multiple_of(b * 256, 256)
        block = feat[:, pl.ds(start, 256)]
        block = jnp.concatenate([block, block[128:]], axis=0)
        turned_block = lax.dot_general(eye, block, (((1,), (1,)), ((), ())), preferred_element_type=jnp.float32)
        table[pl.ds(2 * start, 256, stride=2), :] = turned_block[:, :128]
        table[pl.ds(2 * start + 1, 256, stride=2), :] = turned_block[:, 128:]
        return 0

    feat_copy.wait()
    lax.fori_loop(0, 16, turn, 0)
    for k in range(1, NZ):
        remote(listed.at[z], via.at[lax.rem(z + NZ - k, NZ)], a_send.at[k - 1], a_recv.at[k - 1], near_z[k - 1]).wait_recv()
    for group in range(8):
        for owner in range(8):
            turned[owner, group:group + 1] = via[group, owner:owner + 1]

    def tell(q, _):
        there, seat = plane(q)
        remote(turned.at[there * 2 + seat], asked.at[me], b_send.at[q], b_recv.at[q], plane_at(q)).start()
        return 0

    lax.fori_loop(1, 8, tell, 0)
    asked[me] = turned[me]
    for owner in range(8):
        dest[:, owner * 192:(owner + 1) * 192] = turned[owner][:, :192] >> 13
    lax.fori_loop(16, 32, turn, 0)

    def told(q, _):
        remote(turned.at[0], asked.at[0], b_send.at[q], b_recv.at[q], plane_at(q)).wait_recv()
        return 0

    lax.fori_loop(1, 8, told, 0)
    rows_of[...] = 2 * (asked[...] & 8191).reshape(64, 256)
    copy = pltpu.make_async_copy(rows_of, index, i_sem)
    copy.start()
    copy.wait()

    low_half = lax.broadcasted_iota(jnp.int32, (96, 128), 1) < 64
    low_lane = lax.broadcasted_iota(jnp.int32, (512, 128), 1) < 64

    def fetch(step):
        group = lax.rem(z + order_of(step), NZ)

        def one(i, _):
            turn_of = lax.rem(i, 3)
            q = jnp.where(i < 6, 2 * jnp.where(turn_of == 2, 1, 2 + turn_of) + i // 3, 7 - i)
            there, seat = plane(q)
            line = (there * 2 + seat) * 8 + group

            for s in range(192):
                near[2 * s:2 * s + 2, :] = table[pl.ds(index[line, s], 2), :]
            outgoing[step, q, 0:192] = near[pl.ds(0, 192, stride=2), :].astype(jnp.bfloat16)
            outgoing[step, q, 192:288] = jnp.where(
                low_half, near[pl.ds(1, 96, stride=2), :], near[pl.ds(193, 96, stride=2), :]
            ).astype(jnp.bfloat16)

            @pl.when(q > 0)
            def _():
                remote(outgoing.at[step, q], landed.at[step, me], f_send.at[step, q], f_recv.at[step, q], plane_at(q)).start()

            @pl.when(q == 0)
            def _():
                pltpu.make_async_copy(outgoing.at[step, q], landed.at[step, me], o_sem.at[step]).start()

            return 0

        lax.fori_loop(0, 8, one, 0)

    def gather_in(step):
        group = lax.rem(z + order_of(step), NZ)
        target_id = lax.broadcasted_iota(jnp.int32, (1024, 256), 0)
        for b in range(6):
            choose[:, b * 256:(b + 1) * 256] = jnp.where(
                target_id == dest[pl.ds(group, 1), b * 256:(b + 1) * 256], 1.0, 0.0
            ).astype(jnp.bfloat16)
        pltpu.make_async_copy(outgoing.at[step, 0], landed.at[step, me], o_sem.at[step]).wait()

        def got(q, _):
            remote(outgoing.at[step, q], landed.at[step, me], f_send.at[step, q], f_recv.at[step, q], plane_at(q)).wait_recv()
            return 0

        lax.fori_loop(1, 8, got, 0)
        for owner in range(8):
            base = owner * 192
            held[base:base + 192, 0:128] = landed[step, owner, 0:192]
            pair = landed[step, owner, 192:288]
            held[base:base + 96, 128:256] = pair
            held[base + 96:base + 192, 128:256] = pltpu.roll(pair.astype(jnp.float32), 64, 1).astype(jnp.bfloat16)
        for part in range(4):
            dense[part * 256:(part + 1) * 256] = jnp.dot(
                choose[part * 256:(part + 1) * 256], held[...], preferred_element_type=jnp.float32
            )

    def pieces():
        mixed = jnp.where(low_lane, dense[0:512, 128:256], pltpu.roll(dense[512:1024, 128:256], 64, 1))
        return [dense[0:512, 0:128], mixed, dense[512:1024, 0:128]]

    def ring_at(step):
        up = jnp.logical_or(step == 0, lax.rem(step, 2) == 1)
        return {"wide": wide_at(y, lax.rem(z + jnp.where(up, 1, NZ - 1), NZ), core), "narrow": x}

    def ring_copy(step):
        return remote(ring.at[step], ringed.at[step], r_send.at[step], r_recv.at[step], ring_at(step))

    def pass_on(step):
        @pl.when(jnp.logical_or(step == 0, step == 2))
        def _():
            for i, piece in enumerate(pieces()):
                ring[step, i] = piece.astype(jnp.bfloat16)

        @pl.when(jnp.logical_and(step != 0, step != 2))
        def _():
            before = jnp.where(step == 1, 0, step - 2)
            ring_copy(before).wait_recv()
            for i, piece in enumerate(pieces()):
                ring[step, i] = (piece + ringed[before, i].astype(jnp.float32)).astype(jnp.bfloat16)

        ring_copy(step).start()

    def early(step, _):
        fetch(step)
        return 0

    lax.fori_loop(0, 3, early, 0)

    def loop(step, _):
        @pl.when(step < 5)
        def _():
            fetch(step + 3)

        gather_in(step)
        pass_on(step)
        return 0

    lax.fori_loop(0, 7, loop, 0)
    gather_in(7)
    ring_copy(5).wait_recv()
    ring_copy(6).wait_recv()
    for i, piece in enumerate(pieces()):
        total = piece + ringed[5, i].astype(jnp.float32) + ringed[6, i].astype(jnp.float32)
        if i == 1:
            total = jnp.where(low_lane, total, total / FANOUT)
        if i == 2:
            total = total / FANOUT
        rows[:, i * 128:(i + 1) * 128] = total.astype(jnp.bfloat16)

    middle = jnp.concatenate([ws_ref[128:192], wn_ref[128:192]], axis=0)
    def project(k):
        span = pl.ds(pl.multiple_of(lax.rem(x + k, NX) * 128, 128), 128)
        value = jnp.dot(rows[span, 0:128], ws_ref[0:128], preferred_element_type=jnp.float32)
        value = value + jnp.dot(rows[span, 128:256], middle, preferred_element_type=jnp.float32)
        value = value + jnp.dot(rows[span, 256:384], wn_ref[0:128], preferred_element_type=jnp.float32)
        return value.reshape(2, 64, 256)

    def part_copy(k, h):
        return remote(part_out.at[k - 1, h], got_part.at[k - 1, h], x_send.at[k - 1, h], x_recv.at[k - 1, h], near_x[k - 1])

    sent = []
    for k in (2, 1, 3):
        part_out[k - 1] = project(k).astype(jnp.bfloat16)
        part_copy(k, 0).start()
    for k in (2, 1, 3):
        part_copy(k, 1).start()
        sent += [part_copy(k, 0), part_copy(k, 1)]
    part[...] = project(0)
    for h in range(2):
        value = part[h]
        for k in range(1, NX):
            part_copy(k, h).wait_recv()
            value = value + got_part[k - 1, h].astype(jnp.float32)
        bend = jnp.tanh(ROOT * (value + CUBE * value * value * value))
        rise = 0.5 * (1.0 + bend) + 0.5 * value * (1.0 - bend * bend) * ROOT * (1.0 + 3.0 * CUBE * value * value)
        slopes[x, h] = (cot_ref[h * 64:(h + 1) * 64].astype(jnp.float32) * rise).astype(jnp.bfloat16)
        for k in (2, 1, 3):
            copy = remote(slopes.at[x, h], slopes.at[x, h], s_send.at[k - 1, h], s_recv.at[k - 1, h], near_x[k - 1])
            copy.start()
            sent.append(copy)
        hid_ref[h * 64:(h + 1) * 64] = (0.5 * value * (1.0 + bend)).astype(jnp.bfloat16)
    for k in range(1, NX):
        for h in range(2):
            remote(
                slopes.at[x, h], slopes.at[lax.rem(x + NX - k, NX), h], s_send.at[k - 1, h], s_recv.at[k - 1, h], near_x[k - 1]
            ).wait_recv()
    grads[...] = lax.dot_general(
        rows[...], slopes[...].reshape(512, 256), (((0,), (0,)), ((), ())), preferred_element_type=jnp.float32
    ).reshape(2, NZ, 24, 256)
    copy = remote(grads.at[1 - core], got_core, c_send, c_recv, plane_at(1))
    copy.start()
    sent.append(copy)
    copy.wait_recv()
    full[...] = grads[core] + got_core[...]
    full_out[...] = full[...].astype(jnp.bfloat16)
    for k in range(1, NZ):
        copy = remote(full_out.at[lax.rem(z + k, NZ)], got_z.at[k - 1], z_send.at[k - 1], z_recv.at[k - 1], near_z[k - 1])
        copy.start()
        sent.append(copy)
    mine = full[z]
    for k in range(1, NZ):
        remote(full_out.at[z], got_z.at[k - 1], z_send.at[k - 1], z_recv.at[k - 1], near_z[k - 1]).wait_recv()
        mine = mine + got_z[k - 1].astype(jnp.float32)
    got_y[y] = mine
    for k in range(1, NY):
        copy = remote(got_y.at[y], got_y.at[y], y_send.at[k - 1], y_recv.at[k - 1], plane_at(2 * k))
        copy.start()
        sent.append(copy)
    for k in range(1, NY):
        remote(got_y.at[y], got_y.at[lax.rem(y + NY - k, NY)], y_send.at[k - 1], y_recv.at[k - 1], plane_at(2 * k)).wait_recv()
    final[core, z] = (got_y[0] + got_y[1] + got_y[2] + got_y[3]).astype(jnp.bfloat16)
    for k in range(1, NZ):
        copy = remote(final.at[core, z], final.at[core, z], g_send.at[k - 1], g_recv.at[k - 1], near_z[k - 1])
        copy.start()
        sent.append(copy)
    for k in range(NZ):
        there = lax.rem(z + NZ - k, NZ)
        if k > 0:
            remote(final.at[core, z], final.at[core, there], g_send.at[k - 1], g_recv.at[k - 1], near_z[k - 1]).wait_recv()
        copy = remote(final.at[core, there], final.at[core, there], d_send.at[k], d_recv.at[k], plane_at(1))
        copy.start()
        sent.append(copy)
    for k in range(NZ):
        there = lax.rem(z + NZ - k, NZ)
        remote(final.at[core, z], final.at[1 - core, there], d_send.at[k], d_recv.at[k], plane_at(1)).wait_recv()
    for copy in sent:
        copy.wait_send()

    for k in range(1, NZ):
        remote(listed.at[z], via.at[z], a_send.at[k - 1], a_recv.at[k - 1], near_z[k - 1]).wait_send()

    def drain(q, _):
        remote(turned.at[0], asked.at[0], b_send.at[q], b_recv.at[q], plane_at(q)).wait_send()

        def each(step, _):
            remote(outgoing.at[step, q], landed.at[step, me], f_send.at[step, q], f_recv.at[step, q], plane_at(q)).wait_send()
            return 0

        lax.fori_loop(0, 8, each, 0)
        return 0

    lax.fori_loop(1, 8, drain, 0)

    def drain_ring(step, _):
        ring_copy(step).wait_send()
        return 0

    lax.fori_loop(0, 7, drain_ring, 0)


def finish_kernel(hid_ref, final_ref, out_ref, gs_ref, gn_ref):
    out_ref[...] = hid_ref[...]
    whole = final_ref[...].astype(jnp.float32).reshape(384, 256)
    gs_ref[...] = whole[:192]
    gn_ref[0:128] = whole[256:]
    gn_ref[128:192] = whole[192:256]


def on_device(features, owner_of, row_of, w_self, w_neighbor, cotangent):
    vmem = pl.BlockSpec(memory_space=pltpu.VMEM)
    dma = pltpu.SemaphoreType.DMA
    f32, bf16, i32 = jnp.float32, jnp.bfloat16, jnp.int32
    hidden, final = pl.pallas_call(
        step_kernel,
        out_shape=(jax.ShapeDtypeStruct((128, 256), bf16), jax.ShapeDtypeStruct((2, NZ, 24, 256), bf16)),
        in_specs=[pl.BlockSpec(memory_space=pl.ANY)] + [vmem] * 5,
        out_specs=(vmem, vmem),
        scratch_shapes=[
            pltpu.VMEM((192, 8192), bf16),
            pltpu.VMEM((256, 8192), bf16),
            pltpu.VMEM((192, 8192), bf16),
            pltpu.VMEM((8, 8, 256), i32),
            pltpu.VMEM((8, 8, 256), i32),
            pltpu.VMEM((8, 8, 256), i32),
            pltpu.VMEM((8, 8, 256), i32),
            pltpu.VMEM((64, 256), i32),
            pltpu.SMEM((64, 256), i32),
            pltpu.VMEM((8, 1536), i32),
            pltpu.VMEM((16384, 128), f32),
            pltpu.VMEM((384, 128), f32),
            pltpu.VMEM((8, 8, 288, 128), bf16),
            pltpu.VMEM((8, 8, 288, 128), bf16),
            pltpu.VMEM((1024, 1536), bf16),
            pltpu.VMEM((1536, 256), bf16),
            pltpu.VMEM((1024, 256), f32),
            pltpu.VMEM((7, 3, 512, 128), bf16),
            pltpu.VMEM((7, 3, 512, 128), bf16),
            pltpu.VMEM((512, 384), bf16),
            pltpu.VMEM((2, 64, 256), f32),
            pltpu.VMEM((NX - 1, 2, 64, 256), bf16),
            pltpu.VMEM((NX - 1, 2, 64, 256), bf16),
            pltpu.VMEM((NX, 2, 64, 256), bf16),
            pltpu.VMEM((2, NZ, 24, 256), f32),
            pltpu.VMEM((NZ, 24, 256), f32),
            pltpu.VMEM((NZ, 24, 256), f32),
            pltpu.VMEM((NZ, 24, 256), bf16),
            pltpu.VMEM((NZ - 1, 24, 256), bf16),
            pltpu.VMEM((NY, 24, 256), f32),
            dma(()), dma((NZ - 1,)), dma((NZ - 1,)), dma((8,)), dma((8,)), dma(()),
            dma((8, 8)), dma((8, 8)), dma((8,)), dma((7,)), dma((7,)),
            dma((NX - 1, 2)), dma((NX - 1, 2)), dma((NX - 1, 2)), dma((NX - 1, 2)), dma(()), dma(()),
            dma((NZ - 1,)), dma((NZ - 1,)), dma((NY - 1,)), dma((NY - 1,)),
            dma((NZ - 1,)), dma((NZ - 1,)), dma((NZ,)), dma((NZ,)),
        ],
        compiler_params=pltpu.CompilerParams(
            collective_id=1, has_side_effects=True, vmem_limit_bytes=60 * 1024 * 1024
        ),
        name="step",
    )(features, jnp.transpose(owner_of, (1, 2, 0)), jnp.transpose(row_of), w_self, w_neighbor, cotangent)
    return pl.pallas_call(
        finish_kernel,
        out_shape=(
            jax.ShapeDtypeStruct((128, 256), bf16),
            jax.ShapeDtypeStruct((192, 256), f32),
            jax.ShapeDtypeStruct((192, 256), f32),
        ),
        in_specs=[vmem, vmem],
        out_specs=(vmem, vmem, vmem),
        name="finish",
    )(hidden, final)


def solution(mesh):
    return jax.shard_map(
        on_device,
        mesh=mesh,
        in_specs=(
            P("narrow", "wide"),
            P("wide", None, None),
            P("wide", None),
            P("narrow", None),
            P("narrow", None),
            P(("wide", "narrow"), None),
        ),
        out_specs=(P(("wide", "narrow"), None), P("narrow", None), P("narrow", None)),
        check_vma=False,
    )
```

```python
import jax
import jax.numpy as jnp
from jax import lax
from jax.experimental import pallas as pl
from jax.experimental.pallas import tpu as pltpu
from jax.sharding import PartitionSpec as P

FANOUT = 15
NX, NY, NZ = 4, 4, 8
ROOT, CUBE = 0.7978845608, 0.044715


def remote(src, dst, send, recv, target):
    return pltpu.make_async_remote_copy(
        src_ref=src,
        dst_ref=dst,
        send_sem=send,
        recv_sem=recv,
        device_id=target,
        device_id_type=pl.DeviceIdType.MESH,
    )


def place():
    wide = lax.axis_index("wide")
    return wide // 16, lax.rem(wide // 2, 8), lax.rem(wide, 2), lax.axis_index("narrow")


def wide_at(y, z, core):
    return (y * 8 + z) * 2 + core


def order_of(step):
    odd = lax.rem(step, 2)
    return jnp.where(step == 0, 4, jnp.where(odd == 1, 3 - step // 2, 4 + step // 2))


def list_requests(own_ref, row_ref, listed, stacked, spots):
    upper = (
        lax.broadcasted_iota(jnp.int32, (256, 256), 0) < lax.broadcasted_iota(jnp.int32, (256, 256), 1)
    ).astype(jnp.float32).astype(jnp.bfloat16)
    owner_id = lax.broadcasted_iota(jnp.int32, (64, 512), 0)
    slot_id = lax.broadcasted_iota(jnp.int32, (192, 512), 0)
    lane = lax.broadcasted_iota(jnp.int32, (1, 512), 1)

    def one(j, used):
        owner = own_ref[j]
        row = row_ref[pl.ds(j, 1), :]
        place_of = ((owner >> 1) & 7) * 8 + (owner >> 4) * 2 + (owner & 1)
        mine = owner_id == place_of
        onehot = jnp.where(mine, 1.0, 0.0)
        short = onehot.astype(jnp.bfloat16)
        within = jnp.dot(
            jnp.concatenate([short[:, :256], short[:, 256:]], axis=0), upper, preferred_element_type=jnp.float32
        )
        half = used + jnp.sum(onehot[:, :256], axis=1, keepdims=True)
        before = jnp.concatenate([within[:64] + used, within[64:] + half], axis=1)
        slot = jnp.sum(onehot * before, axis=0, keepdims=True).astype(jnp.int32)
        span = pl.ds(pl.multiple_of(j * 512, 512), 512)
        spots[:, span] = jnp.where(slot_id == slot, 1.0, 0.0).astype(jnp.bfloat16)
        for i, piece in enumerate([row & 255, row >> 8, lane & 255, (lane >> 8) + 2 * j + 1]):
            stacked[i * 64:(i + 1) * 64, span] = short * piece.astype(jnp.float32).astype(jnp.bfloat16)
        return half + jnp.sum(onehot[:, 256:], axis=1, keepdims=True)

    lax.fori_loop(0, 16, one, jnp.zeros((64, 1), jnp.float32), unroll=4)
    found = lax.dot_general(
        stacked[...], spots[...], (((1,), (1,)), ((), ())), preferred_element_type=jnp.float32
    )
    found = found.astype(jnp.int32)
    row = found[0:64] + 256 * found[64:128]
    block = found[192:256]
    item = found[128:192] + 256 * (block - 1)
    target = jnp.where(block > 0, jnp.where(item < 512, item, 512 + (item & 511)), 1024)
    listed[...] = jnp.zeros_like(listed)
    listed[:, :, 0:192] = (row + 8192 * target).reshape(8, 8, 192)


def step_kernel(
    feat_ref, own_ref, row_ref, ws_ref, wn_ref, cot_ref, hid_ref, final,
    feat, stacked, spots, listed, via, turned, asked, rows_of, index, dest, table, near, outgoing, landed, choose, held, dense, ring, ringed,
    rows, part, part_out, got_part, slopes, grads, got_core, full, full_out, got_z, got_y,
    e_sem, a_send, a_recv, b_send, b_recv, i_sem, f_send, f_recv, o_sem, r_send, r_recv,
    x_send, x_recv, s_send, s_recv, c_send, c_recv, z_send, z_recv, y_send, y_recv, g_send, g_recv, d_send, d_recv,
):
    y, z, core, x = place()
    near_z = [{"wide": wide_at(y, lax.rem(z + k, NZ), core), "narrow": x} for k in range(1, NZ)]
    near_x = [{"wide": wide_at(y, z, core), "narrow": lax.rem(x + k, NX)} for k in range(1, NX)]

    def plane(q):
        return lax.rem(y + q // 2, NY), lax.rem(core + q, 2)

    def plane_at(q):
        there, seat = plane(q)
        return {"wide": wide_at(there, z, seat), "narrow": x}

    barrier = pltpu.get_barrier_semaphore()
    targets = near_z + [plane_at(q) for q in range(1, 8)] + near_x
    for target in targets:
        pl.semaphore_signal(barrier, inc=1, device_id=target, device_id_type=pl.DeviceIdType.MESH)
    feat_copy = pltpu.make_async_copy(feat_ref, feat, e_sem)
    feat_copy.start()
    me = y * 2 + core

    list_requests(own_ref, row_ref, listed, stacked, spots)
    pl.semaphore_wait(barrier, len(targets))
    for k in range(1, NZ):
        remote(listed.at[lax.rem(z + k, NZ)], via.at[z], a_send.at[k - 1], a_recv.at[k - 1], near_z[k - 1]).start()
    via[z] = listed[z]

    eye = (
        lax.broadcasted_iota(jnp.int32, (256, 256), 0) == lax.broadcasted_iota(jnp.int32, (256, 256), 1)
    ).astype(jnp.float32).astype(jnp.bfloat16)

    def turn(b, _):
        start = pl.multiple_of(b * 256, 256)
        block = feat[:, pl.ds(start, 256)]
        block = jnp.concatenate([block, block[128:]], axis=0)
        turned_block = lax.dot_general(eye, block, (((1,), (1,)), ((), ())), preferred_element_type=jnp.float32)
        table[pl.ds(2 * start, 256, stride=2), :] = turned_block[:, :128]
        table[pl.ds(2 * start + 1, 256, stride=2), :] = turned_block[:, 128:]
        return 0

    feat_copy.wait()
    lax.fori_loop(0, 16, turn, 0)
    for k in range(1, NZ):
        remote(listed.at[z], via.at[lax.rem(z + NZ - k, NZ)], a_send.at[k - 1], a_recv.at[k - 1], near_z[k - 1]).wait_recv()
    for group in range(8):
        for owner in range(8):
            turned[owner, group:group + 1] = via[group, owner:owner + 1]

    def tell(q, _):
        there, seat = plane(q)
        remote(turned.at[there * 2 + seat], asked.at[me], b_send.at[q], b_recv.at[q], plane_at(q)).start()
        return 0

    lax.fori_loop(1, 8, tell, 0)
    asked[me] = turned[me]
    for owner in range(8):
        dest[:, owner * 192:(owner + 1) * 192] = turned[owner][:, :192] >> 13
    lax.fori_loop(16, 32, turn, 0)

    def told(q, _):
        remote(turned.at[0], asked.at[0], b_send.at[q], b_recv.at[q], plane_at(q)).wait_recv()
        return 0

    lax.fori_loop(1, 8, told, 0)
    for group in range(8):
        rows_of[group] = 2 * (asked[:, group] & 8191)

    def index_copy(step):
        group = lax.rem(z + order_of(step), NZ)
        return pltpu.make_async_copy(
            rows_of.at[group], index.at[pl.ds(pl.multiple_of(group * 8, 8), 8)], i_sem.at[step]
        )

    def take(step, _):
        index_copy(step).start()
        return 0

    lax.fori_loop(0, 8, take, 0)

    low_half = lax.broadcasted_iota(jnp.int32, (96, 128), 1) < 64
    low_lane = lax.broadcasted_iota(jnp.int32, (512, 128), 1) < 64

    def fetch(step):
        group = lax.rem(z + order_of(step), NZ)
        index_copy(step).wait()

        def one(i, _):
            turn_of = lax.rem(i, 3)
            q = jnp.where(i < 6, 2 * jnp.where(turn_of == 2, 1, 2 + turn_of) + i // 3, 7 - i)
            there, seat = plane(q)
            line = group * 8 + there * 2 + seat

            for s in range(192):
                near[2 * s:2 * s + 2, :] = table[pl.ds(index[line, s], 2), :]
            outgoing[step, q, 0:192] = near[pl.ds(0, 192, stride=2), :].astype(jnp.bfloat16)
            outgoing[step, q, 192:288] = jnp.where(
                low_half, near[pl.ds(1, 96, stride=2), :], near[pl.ds(193, 96, stride=2), :]
            ).astype(jnp.bfloat16)

            @pl.when(q > 0)
            def _():
                remote(outgoing.at[step, q], landed.at[step, me], f_send.at[step, q], f_recv.at[step, q], plane_at(q)).start()

            @pl.when(q == 0)
            def _():
                pltpu.make_async_copy(outgoing.at[step, q], landed.at[step, me], o_sem.at[step]).start()

            return 0

        lax.fori_loop(0, 8, one, 0)

    def gather_in(step):
        group = lax.rem(z + order_of(step), NZ)
        target_id = lax.broadcasted_iota(jnp.int32, (1024, 256), 0)
        for b in range(6):
            choose[:, b * 256:(b + 1) * 256] = jnp.where(
                target_id == dest[pl.ds(group, 1), b * 256:(b + 1) * 256], 1.0, 0.0
            ).astype(jnp.bfloat16)
        pltpu.make_async_copy(outgoing.at[step, 0], landed.at[step, me], o_sem.at[step]).wait()

        def got(q, _):
            remote(outgoing.at[step, q], landed.at[step, me], f_send.at[step, q], f_recv.at[step, q], plane_at(q)).wait_recv()
            return 0

        lax.fori_loop(1, 8, got, 0)
        for owner in range(8):
            base = owner * 192
            held[base:base + 192, 0:128] = landed[step, owner, 0:192]
            pair = landed[step, owner, 192:288]
            held[base:base + 96, 128:256] = pair
            held[base + 96:base + 192, 128:256] = pltpu.roll(pair.astype(jnp.float32), 64, 1).astype(jnp.bfloat16)
        for part in range(4):
            dense[part * 256:(part + 1) * 256] = jnp.dot(
                choose[part * 256:(part + 1) * 256], held[...], preferred_element_type=jnp.float32
            )

    def pieces():
        mixed = jnp.where(low_lane, dense[0:512, 128:256], pltpu.roll(dense[512:1024, 128:256], 64, 1))
        return [dense[0:512, 0:128], mixed, dense[512:1024, 0:128]]

    def ring_at(step):
        up = jnp.logical_or(step == 0, lax.rem(step, 2) == 1)
        return {"wide": wide_at(y, lax.rem(z + jnp.where(up, 1, NZ - 1), NZ), core), "narrow": x}

    def ring_copy(step):
        return remote(ring.at[step], ringed.at[step], r_send.at[step], r_recv.at[step], ring_at(step))

    def pass_on(step):
        @pl.when(jnp.logical_or(step == 0, step == 2))
        def _():
            for i, piece in enumerate(pieces()):
                ring[step, i] = piece.astype(jnp.bfloat16)

        @pl.when(jnp.logical_and(step != 0, step != 2))
        def _():
            before = jnp.where(step == 1, 0, step - 2)
            ring_copy(before).wait_recv()
            for i, piece in enumerate(pieces()):
                ring[step, i] = (piece + ringed[before, i].astype(jnp.float32)).astype(jnp.bfloat16)

        ring_copy(step).start()

    def early(step, _):
        fetch(step)
        return 0

    lax.fori_loop(0, 3, early, 0)

    def loop(step, _):
        @pl.when(step < 5)
        def _():
            fetch(step + 3)

        gather_in(step)
        pass_on(step)
        return 0

    lax.fori_loop(0, 7, loop, 0)
    gather_in(7)
    ring_copy(5).wait_recv()
    ring_copy(6).wait_recv()
    for i, piece in enumerate(pieces()):
        total = piece + ringed[5, i].astype(jnp.float32) + ringed[6, i].astype(jnp.float32)
        if i == 1:
            total = jnp.where(low_lane, total, total / FANOUT)
        if i == 2:
            total = total / FANOUT
        rows[:, i * 128:(i + 1) * 128] = total.astype(jnp.bfloat16)

    middle = jnp.concatenate([ws_ref[128:192], wn_ref[128:192]], axis=0)
    def project(k):
        span = pl.ds(pl.multiple_of(lax.rem(x + k, NX) * 128, 128), 128)
        value = jnp.dot(rows[span, 0:128], ws_ref[0:128], preferred_element_type=jnp.float32)
        value = value + jnp.dot(rows[span, 128:256], middle, preferred_element_type=jnp.float32)
        value = value + jnp.dot(rows[span, 256:384], wn_ref[0:128], preferred_element_type=jnp.float32)
        return value.reshape(2, 64, 256)

    def part_copy(k, h):
        return remote(part_out.at[k - 1, h], got_part.at[k - 1, h], x_send.at[k - 1, h], x_recv.at[k - 1, h], near_x[k - 1])

    sent = []
    for k in (2, 1, 3):
        part_out[k - 1] = project(k).astype(jnp.bfloat16)
        part_copy(k, 0).start()
    for k in (2, 1, 3):
        part_copy(k, 1).start()
        sent += [part_copy(k, 0), part_copy(k, 1)]
    part[...] = project(0)
    for h in range(2):
        value = part[h]
        for k in range(1, NX):
            part_copy(k, h).wait_recv()
            value = value + got_part[k - 1, h].astype(jnp.float32)
        bend = jnp.tanh(ROOT * (value + CUBE * value * value * value))
        rise = 0.5 * (1.0 + bend) + 0.5 * value * (1.0 - bend * bend) * ROOT * (1.0 + 3.0 * CUBE * value * value)
        slopes[x, h] = (cot_ref[h * 64:(h + 1) * 64].astype(jnp.float32) * rise).astype(jnp.bfloat16)
        for k in (2, 1, 3):
            copy = remote(slopes.at[x, h], slopes.at[x, h], s_send.at[k - 1, h], s_recv.at[k - 1, h], near_x[k - 1])
            copy.start()
            sent.append(copy)
        hid_ref[h * 64:(h + 1) * 64] = (0.5 * value * (1.0 + bend)).astype(jnp.bfloat16)
    for k in range(1, NX):
        for h in range(2):
            remote(
                slopes.at[x, h], slopes.at[lax.rem(x + NX - k, NX), h], s_send.at[k - 1, h], s_recv.at[k - 1, h], near_x[k - 1]
            ).wait_recv()
    grads[...] = lax.dot_general(
        rows[...], slopes[...].reshape(512, 256), (((0,), (0,)), ((), ())), preferred_element_type=jnp.float32
    ).reshape(2, NZ, 24, 256)
    copy = remote(grads.at[1 - core], got_core, c_send, c_recv, plane_at(1))
    copy.start()
    sent.append(copy)
    copy.wait_recv()
    full[...] = grads[core] + got_core[...]
    full_out[...] = full[...].astype(jnp.bfloat16)
    for k in range(1, NZ):
        copy = remote(full_out.at[lax.rem(z + k, NZ)], got_z.at[k - 1], z_send.at[k - 1], z_recv.at[k - 1], near_z[k - 1])
        copy.start()
        sent.append(copy)
    mine = full[z]
    for k in range(1, NZ):
        remote(full_out.at[z], got_z.at[k - 1], z_send.at[k - 1], z_recv.at[k - 1], near_z[k - 1]).wait_recv()
        mine = mine + got_z[k - 1].astype(jnp.float32)
    got_y[y] = mine
    for k in range(1, NY):
        copy = remote(got_y.at[y], got_y.at[y], y_send.at[k - 1], y_recv.at[k - 1], plane_at(2 * k))
        copy.start()
        sent.append(copy)
    for k in range(1, NY):
        remote(got_y.at[y], got_y.at[lax.rem(y + NY - k, NY)], y_send.at[k - 1], y_recv.at[k - 1], plane_at(2 * k)).wait_recv()
    final[core, z] = (got_y[0] + got_y[1] + got_y[2] + got_y[3]).astype(jnp.bfloat16)
    for k in range(1, NZ):
        copy = remote(final.at[core, z], final.at[core, z], g_send.at[k - 1], g_recv.at[k - 1], near_z[k - 1])
        copy.start()
        sent.append(copy)
    for k in range(NZ):
        there = lax.rem(z + NZ - k, NZ)
        if k > 0:
            remote(final.at[core, z], final.at[core, there], g_send.at[k - 1], g_recv.at[k - 1], near_z[k - 1]).wait_recv()
        copy = remote(final.at[core, there], final.at[core, there], d_send.at[k], d_recv.at[k], plane_at(1))
        copy.start()
        sent.append(copy)
    for k in range(NZ):
        there = lax.rem(z + NZ - k, NZ)
        remote(final.at[core, z], final.at[1 - core, there], d_send.at[k], d_recv.at[k], plane_at(1)).wait_recv()
    for copy in sent:
        copy.wait_send()

    for k in range(1, NZ):
        remote(listed.at[z], via.at[z], a_send.at[k - 1], a_recv.at[k - 1], near_z[k - 1]).wait_send()

    def drain(q, _):
        remote(turned.at[0], asked.at[0], b_send.at[q], b_recv.at[q], plane_at(q)).wait_send()

        def each(step, _):
            remote(outgoing.at[step, q], landed.at[step, me], f_send.at[step, q], f_recv.at[step, q], plane_at(q)).wait_send()
            return 0

        lax.fori_loop(0, 8, each, 0)
        return 0

    lax.fori_loop(1, 8, drain, 0)

    def drain_ring(step, _):
        ring_copy(step).wait_send()
        return 0

    lax.fori_loop(0, 7, drain_ring, 0)


def finish_kernel(hid_ref, final_ref, out_ref, gs_ref, gn_ref):
    out_ref[...] = hid_ref[...]
    whole = final_ref[...].astype(jnp.float32).reshape(384, 256)
    gs_ref[...] = whole[:192]
    gn_ref[0:128] = whole[256:]
    gn_ref[128:192] = whole[192:256]


def on_device(features, owner_of, row_of, w_self, w_neighbor, cotangent):
    vmem = pl.BlockSpec(memory_space=pltpu.VMEM)
    dma = pltpu.SemaphoreType.DMA
    f32, bf16, i32 = jnp.float32, jnp.bfloat16, jnp.int32
    hidden, final = pl.pallas_call(
        step_kernel,
        out_shape=(jax.ShapeDtypeStruct((128, 256), bf16), jax.ShapeDtypeStruct((2, NZ, 24, 256), bf16)),
        in_specs=[pl.BlockSpec(memory_space=pl.ANY)] + [vmem] * 5,
        out_specs=(vmem, vmem),
        scratch_shapes=[
            pltpu.VMEM((192, 8192), bf16),
            pltpu.VMEM((256, 8192), bf16),
            pltpu.VMEM((192, 8192), bf16),
            pltpu.VMEM((8, 8, 256), i32),
            pltpu.VMEM((8, 8, 256), i32),
            pltpu.VMEM((8, 8, 256), i32),
            pltpu.VMEM((8, 8, 256), i32),
            pltpu.VMEM((8, 8, 256), i32),
            pltpu.SMEM((64, 256), i32),
            pltpu.VMEM((8, 1536), i32),
            pltpu.VMEM((16384, 128), f32),
            pltpu.VMEM((384, 128), f32),
            pltpu.VMEM((8, 8, 288, 128), bf16),
            pltpu.VMEM((8, 8, 288, 128), bf16),
            pltpu.VMEM((1024, 1536), bf16),
            pltpu.VMEM((1536, 256), bf16),
            pltpu.VMEM((1024, 256), f32),
            pltpu.VMEM((7, 3, 512, 128), bf16),
            pltpu.VMEM((7, 3, 512, 128), bf16),
            pltpu.VMEM((512, 384), bf16),
            pltpu.VMEM((2, 64, 256), f32),
            pltpu.VMEM((NX - 1, 2, 64, 256), bf16),
            pltpu.VMEM((NX - 1, 2, 64, 256), bf16),
            pltpu.VMEM((NX, 2, 64, 256), bf16),
            pltpu.VMEM((2, NZ, 24, 256), f32),
            pltpu.VMEM((NZ, 24, 256), f32),
            pltpu.VMEM((NZ, 24, 256), f32),
            pltpu.VMEM((NZ, 24, 256), bf16),
            pltpu.VMEM((NZ - 1, 24, 256), bf16),
            pltpu.VMEM((NY, 24, 256), f32),
            dma(()), dma((NZ - 1,)), dma((NZ - 1,)), dma((8,)), dma((8,)), dma((8,)),
            dma((8, 8)), dma((8, 8)), dma((8,)), dma((7,)), dma((7,)),
            dma((NX - 1, 2)), dma((NX - 1, 2)), dma((NX - 1, 2)), dma((NX - 1, 2)), dma(()), dma(()),
            dma((NZ - 1,)), dma((NZ - 1,)), dma((NY - 1,)), dma((NY - 1,)),
            dma((NZ - 1,)), dma((NZ - 1,)), dma((NZ,)), dma((NZ,)),
        ],
        compiler_params=pltpu.CompilerParams(
            collective_id=1, has_side_effects=True, vmem_limit_bytes=60 * 1024 * 1024
        ),
        name="step",
    )(features, jnp.transpose(owner_of, (1, 2, 0)), jnp.transpose(row_of), w_self, w_neighbor, cotangent)
    return pl.pallas_call(
        finish_kernel,
        out_shape=(
            jax.ShapeDtypeStruct((128, 256), bf16),
            jax.ShapeDtypeStruct((192, 256), f32),
            jax.ShapeDtypeStruct((192, 256), f32),
        ),
        in_specs=[vmem, vmem],
        out_specs=(vmem, vmem, vmem),
        name="finish",
    )(hidden, final)


def solution(mesh):
    return jax.shard_map(
        on_device,
        mesh=mesh,
        in_specs=(
            P("narrow", "wide"),
            P("wide", None, None),
            P("wide", None),
            P("narrow", None),
            P("narrow", None),
            P(("wide", "narrow"), None),
        ),
        out_specs=(P(("wide", "narrow"), None), P("narrow", None), P("narrow", None)),
        check_vma=False,
    )
```

```python
import jax
import jax.numpy as jnp
from jax import lax
from jax.experimental import pallas as pl
from jax.experimental.pallas import tpu as pltpu
from jax.sharding import PartitionSpec as P

FANOUT = 15
NX, NY, NZ = 4, 4, 8
ROOT, CUBE = 0.7978845608, 0.044715


def remote(src, dst, send, recv, target):
    return pltpu.make_async_remote_copy(
        src_ref=src,
        dst_ref=dst,
        send_sem=send,
        recv_sem=recv,
        device_id=target,
        device_id_type=pl.DeviceIdType.MESH,
    )


def place():
    wide = lax.axis_index("wide")
    return wide // 16, lax.rem(wide // 2, 8), lax.rem(wide, 2), lax.axis_index("narrow")


def wide_at(y, z, core):
    return (y * 8 + z) * 2 + core


def order_of(step):
    odd = lax.rem(step, 2)
    return jnp.where(step == 0, 4, jnp.where(odd == 1, 3 - step // 2, 4 + step // 2))


def list_requests(own_ref, row_ref, listed, stacked, spots):
    upper = (
        lax.broadcasted_iota(jnp.int32, (256, 256), 0) < lax.broadcasted_iota(jnp.int32, (256, 256), 1)
    ).astype(jnp.float32).astype(jnp.bfloat16)
    owner_id = lax.broadcasted_iota(jnp.int32, (64, 512), 0)
    slot_id = lax.broadcasted_iota(jnp.int32, (192, 512), 0)
    lane = lax.broadcasted_iota(jnp.int32, (1, 512), 1)

    def one(j, used):
        owner = own_ref[j]
        row = row_ref[pl.ds(j, 1), :]
        place_of = ((owner >> 1) & 7) * 8 + (owner >> 4) * 2 + (owner & 1)
        mine = owner_id == place_of
        onehot = jnp.where(mine, 1.0, 0.0)
        short = onehot.astype(jnp.bfloat16)
        within = jnp.dot(
            jnp.concatenate([short[:, :256], short[:, 256:]], axis=0), upper, preferred_element_type=jnp.float32
        )
        half = used + jnp.sum(onehot[:, :256], axis=1, keepdims=True)
        before = jnp.concatenate([within[:64] + used, within[64:] + half], axis=1)
        slot = jnp.sum(onehot * before, axis=0, keepdims=True).astype(jnp.int32)
        span = pl.ds(pl.multiple_of(j * 512, 512), 512)
        spots[:, span] = jnp.where(slot_id == slot, 1.0, 0.0).astype(jnp.bfloat16)
        for i, piece in enumerate([row & 255, row >> 8, lane & 255, (lane >> 8) + 2 * j + 1]):
            stacked[i * 64:(i + 1) * 64, span] = short * piece.astype(jnp.float32).astype(jnp.bfloat16)
        return half + jnp.sum(onehot[:, 256:], axis=1, keepdims=True)

    lax.fori_loop(0, 16, one, jnp.zeros((64, 1), jnp.float32), unroll=4)
    found = lax.dot_general(
        stacked[...], spots[...], (((1,), (1,)), ((), ())), preferred_element_type=jnp.float32
    )
    found = found.astype(jnp.int32)
    row = found[0:64] + 256 * found[64:128]
    block = found[192:256]
    item = found[128:192] + 256 * (block - 1)
    target = jnp.where(block > 0, jnp.where(item < 512, item, 512 + (item & 511)), 1024)
    listed[...] = jnp.zeros_like(listed)
    listed[:, :, 0:192] = (row + 8192 * target).reshape(8, 8, 192)


def step_kernel(
    feat_ref, own_ref, row_ref, ws_ref, wn_ref, cot_ref, hid_ref, final,
    feat, stacked, spots, listed, via, turned, asked, rows_of, index, dest, table, near, outgoing, landed, choose, held, dense, ring, ringed,
    rows, rows_turned, part, part_out, got_part, slopes, grads, got_core, full, full_out, got_z, got_y,
    e_sem, a_send, a_recv, b_send, b_recv, i_sem, f_send, f_recv, o_sem, r_send, r_recv,
    x_send, x_recv, s_send, s_recv, c_send, c_recv, z_send, z_recv, y_send, y_recv, g_send, g_recv, d_send, d_recv,
):
    y, z, core, x = place()
    near_z = [{"wide": wide_at(y, lax.rem(z + k, NZ), core), "narrow": x} for k in range(1, NZ)]
    near_x = [{"wide": wide_at(y, z, core), "narrow": lax.rem(x + k, NX)} for k in range(1, NX)]

    def plane(q):
        return lax.rem(y + q // 2, NY), lax.rem(core + q, 2)

    def plane_at(q):
        there, seat = plane(q)
        return {"wide": wide_at(there, z, seat), "narrow": x}

    barrier = pltpu.get_barrier_semaphore()
    targets = near_z + [plane_at(q) for q in range(1, 8)] + near_x
    for target in targets:
        pl.semaphore_signal(barrier, inc=1, device_id=target, device_id_type=pl.DeviceIdType.MESH)
    feat_copy = pltpu.make_async_copy(feat_ref, feat, e_sem)
    feat_copy.start()
    me = y * 2 + core

    list_requests(own_ref, row_ref, listed, stacked, spots)
    pl.semaphore_wait(barrier, len(targets))
    for k in range(1, NZ):
        remote(listed.at[lax.rem(z + k, NZ)], via.at[z], a_send.at[k - 1], a_recv.at[k - 1], near_z[k - 1]).start()
    via[z] = listed[z]

    eye = (
        lax.broadcasted_iota(jnp.int32, (256, 256), 0) == lax.broadcasted_iota(jnp.int32, (256, 256), 1)
    ).astype(jnp.float32).astype(jnp.bfloat16)

    def turn(b, _):
        start = pl.multiple_of(b * 256, 256)
        block = feat[:, pl.ds(start, 256)]
        block = jnp.concatenate([block, block[128:]], axis=0)
        turned_block = lax.dot_general(eye, block, (((1,), (1,)), ((), ())), preferred_element_type=jnp.float32)
        table[pl.ds(2 * start, 256, stride=2), :] = turned_block[:, :128]
        table[pl.ds(2 * start + 1, 256, stride=2), :] = turned_block[:, 128:]
        return 0

    feat_copy.wait()
    lax.fori_loop(0, 16, turn, 0)
    for k in range(1, NZ):
        remote(listed.at[z], via.at[lax.rem(z + NZ - k, NZ)], a_send.at[k - 1], a_recv.at[k - 1], near_z[k - 1]).wait_recv()
    for group in range(8):
        for owner in range(8):
            turned[owner, group:group + 1] = via[group, owner:owner + 1]

    def tell(q, _):
        there, seat = plane(q)
        remote(turned.at[there * 2 + seat], asked.at[me], b_send.at[q], b_recv.at[q], plane_at(q)).start()
        return 0

    lax.fori_loop(1, 8, tell, 0)
    asked[me] = turned[me]
    for owner in range(8):
        dest[:, owner * 192:(owner + 1) * 192] = turned[owner][:, :192] >> 13
    lax.fori_loop(16, 32, turn, 0)

    def told(q, _):
        remote(turned.at[0], asked.at[0], b_send.at[q], b_recv.at[q], plane_at(q)).wait_recv()
        return 0

    lax.fori_loop(1, 8, told, 0)
    for group in range(8):
        rows_of[group] = 2 * (asked[:, group] & 8191)

    def index_copy(step):
        group = lax.rem(z + order_of(step), NZ)
        return pltpu.make_async_copy(
            rows_of.at[group], index.at[pl.ds(pl.multiple_of(group * 8, 8), 8)], i_sem.at[step]
        )

    def take(step, _):
        index_copy(step).start()
        return 0

    lax.fori_loop(0, 8, take, 0)

    low_half = lax.broadcasted_iota(jnp.int32, (96, 128), 1) < 64
    low_lane = lax.broadcasted_iota(jnp.int32, (512, 128), 1) < 64

    def fetch(step):
        group = lax.rem(z + order_of(step), NZ)
        index_copy(step).wait()

        def one(i, _):
            turn_of = lax.rem(i, 3)
            q = jnp.where(i < 6, 2 * jnp.where(turn_of == 2, 1, 2 + turn_of) + i // 3, 7 - i)
            there, seat = plane(q)
            line = group * 8 + there * 2 + seat

            for s in range(192):
                near[2 * s:2 * s + 2, :] = table[pl.ds(index[line, s], 2), :]
            outgoing[step, q, 0:192] = near[pl.ds(0, 192, stride=2), :].astype(jnp.bfloat16)
            outgoing[step, q, 192:288] = jnp.where(
                low_half, near[pl.ds(1, 96, stride=2), :], near[pl.ds(193, 96, stride=2), :]
            ).astype(jnp.bfloat16)

            @pl.when(q > 0)
            def _():
                remote(outgoing.at[step, q], landed.at[step, me], f_send.at[step, q], f_recv.at[step, q], plane_at(q)).start()

            @pl.when(q == 0)
            def _():
                pltpu.make_async_copy(outgoing.at[step, q], landed.at[step, me], o_sem.at[step]).start()

            return 0

        lax.fori_loop(0, 8, one, 0)

    def gather_in(step):
        group = lax.rem(z + order_of(step), NZ)
        target_id = lax.broadcasted_iota(jnp.int32, (1024, 256), 0)
        for b in range(6):
            choose[:, b * 256:(b + 1) * 256] = jnp.where(
                target_id == dest[pl.ds(group, 1), b * 256:(b + 1) * 256], 1.0, 0.0
            ).astype(jnp.bfloat16)
        pltpu.make_async_copy(outgoing.at[step, 0], landed.at[step, me], o_sem.at[step]).wait()

        def got(q, _):
            remote(outgoing.at[step, q], landed.at[step, me], f_send.at[step, q], f_recv.at[step, q], plane_at(q)).wait_recv()
            return 0

        lax.fori_loop(1, 8, got, 0)
        for owner in range(8):
            base = owner * 192
            held[base:base + 192, 0:128] = landed[step, owner, 0:192]
            pair = landed[step, owner, 192:288]
            held[base:base + 96, 128:256] = pair
            held[base + 96:base + 192, 128:256] = pltpu.roll(pair.astype(jnp.float32), 64, 1).astype(jnp.bfloat16)
        for part in range(4):
            dense[part * 256:(part + 1) * 256] = jnp.dot(
                choose[part * 256:(part + 1) * 256], held[...], preferred_element_type=jnp.float32
            )

    def pieces():
        mixed = jnp.where(low_lane, dense[0:512, 128:256], pltpu.roll(dense[512:1024, 128:256], 64, 1))
        return [dense[0:512, 0:128], mixed, dense[512:1024, 0:128]]

    def ring_at(step):
        up = jnp.logical_or(step == 0, lax.rem(step, 2) == 1)
        return {"wide": wide_at(y, lax.rem(z + jnp.where(up, 1, NZ - 1), NZ), core), "narrow": x}

    def ring_copy(step):
        return remote(ring.at[step], ringed.at[step], r_send.at[step], r_recv.at[step], ring_at(step))

    def pass_on(step):
        @pl.when(jnp.logical_or(step == 0, step == 2))
        def _():
            for i, piece in enumerate(pieces()):
                ring[step, i] = piece.astype(jnp.bfloat16)

        @pl.when(jnp.logical_and(step != 0, step != 2))
        def _():
            before = jnp.where(step == 1, 0, step - 2)
            ring_copy(before).wait_recv()
            for i, piece in enumerate(pieces()):
                ring[step, i] = (piece + ringed[before, i].astype(jnp.float32)).astype(jnp.bfloat16)

        ring_copy(step).start()

    def early(step, _):
        fetch(step)
        return 0

    lax.fori_loop(0, 3, early, 0)

    def loop(step, _):
        @pl.when(step < 5)
        def _():
            fetch(step + 3)

        gather_in(step)
        pass_on(step)
        return 0

    lax.fori_loop(0, 7, loop, 0)
    gather_in(7)
    ring_copy(5).wait_recv()
    ring_copy(6).wait_recv()
    for i, piece in enumerate(pieces()):
        total = piece + ringed[5, i].astype(jnp.float32) + ringed[6, i].astype(jnp.float32)
        if i == 1:
            total = jnp.where(low_lane, total, total / FANOUT)
        if i == 2:
            total = total / FANOUT
        rows[:, i * 128:(i + 1) * 128] = total.astype(jnp.bfloat16)

    middle = jnp.concatenate([ws_ref[128:192], wn_ref[128:192]], axis=0)
    def project(k):
        span = pl.ds(pl.multiple_of(lax.rem(x + k, NX) * 128, 128), 128)
        value = jnp.dot(rows[span, 0:128], ws_ref[0:128], preferred_element_type=jnp.float32)
        value = value + jnp.dot(rows[span, 128:256], middle, preferred_element_type=jnp.float32)
        value = value + jnp.dot(rows[span, 256:384], wn_ref[0:128], preferred_element_type=jnp.float32)
        return value.reshape(2, 64, 256)

    def part_copy(k, h):
        return remote(part_out.at[k - 1, h], got_part.at[k - 1, h], x_send.at[k - 1, h], x_recv.at[k - 1, h], near_x[k - 1])

    sent = []
    for k in (2, 1, 3):
        part_out[k - 1] = project(k).astype(jnp.bfloat16)
        part_copy(k, 0).start()
    for k in (2, 1, 3):
        part_copy(k, 1).start()
        sent += [part_copy(k, 0), part_copy(k, 1)]
    part[...] = project(0)
    rows_turned[...] = rows[...].T
    for h in range(2):
        value = part[h]
        for k in range(1, NX):
            part_copy(k, h).wait_recv()
            value = value + got_part[k - 1, h].astype(jnp.float32)
        bend = jnp.tanh(ROOT * (value + CUBE * value * value * value))
        rise = 0.5 * (1.0 + bend) + 0.5 * value * (1.0 - bend * bend) * ROOT * (1.0 + 3.0 * CUBE * value * value)
        slopes[x, h] = (cot_ref[h * 64:(h + 1) * 64].astype(jnp.float32) * rise).astype(jnp.bfloat16)
        for k in (2, 1, 3):
            copy = remote(slopes.at[x, h], slopes.at[x, h], s_send.at[k - 1, h], s_recv.at[k - 1, h], near_x[k - 1])
            copy.start()
            sent.append(copy)
        hid_ref[h * 64:(h + 1) * 64] = (0.5 * value * (1.0 + bend)).astype(jnp.bfloat16)
    for k in range(1, NX):
        for h in range(2):
            remote(
                slopes.at[x, h], slopes.at[lax.rem(x + NX - k, NX), h], s_send.at[k - 1, h], s_recv.at[k - 1, h], near_x[k - 1]
            ).wait_recv()
    grads[...] = jnp.dot(
        rows_turned[...], slopes[...].reshape(512, 256), preferred_element_type=jnp.float32
    ).reshape(2, NZ, 24, 256)
    copy = remote(grads.at[1 - core], got_core, c_send, c_recv, plane_at(1))
    copy.start()
    sent.append(copy)
    copy.wait_recv()
    full[...] = grads[core] + got_core[...]
    full_out[...] = full[...].astype(jnp.bfloat16)
    for k in range(1, NZ):
        copy = remote(full_out.at[lax.rem(z + k, NZ)], got_z.at[k - 1], z_send.at[k - 1], z_recv.at[k - 1], near_z[k - 1])
        copy.start()
        sent.append(copy)
    for k in range(1, NZ):
        remote(listed.at[z], via.at[z], a_send.at[k - 1], a_recv.at[k - 1], near_z[k - 1]).wait_send()

    def drain(q, _):
        remote(turned.at[0], asked.at[0], b_send.at[q], b_recv.at[q], plane_at(q)).wait_send()

        def each(step, _):
            remote(outgoing.at[step, q], landed.at[step, me], f_send.at[step, q], f_recv.at[step, q], plane_at(q)).wait_send()
            return 0

        lax.fori_loop(0, 8, each, 0)
        return 0

    lax.fori_loop(1, 8, drain, 0)

    def drain_ring(step, _):
        ring_copy(step).wait_send()
        return 0

    lax.fori_loop(0, 7, drain_ring, 0)

    mine = full[z]
    for k in range(1, NZ):
        remote(full_out.at[z], got_z.at[k - 1], z_send.at[k - 1], z_recv.at[k - 1], near_z[k - 1]).wait_recv()
        mine = mine + got_z[k - 1].astype(jnp.float32)
    got_y[y] = mine
    for k in range(1, NY):
        copy = remote(got_y.at[y], got_y.at[y], y_send.at[k - 1], y_recv.at[k - 1], plane_at(2 * k))
        copy.start()
        sent.append(copy)
    for k in range(1, NY):
        remote(got_y.at[y], got_y.at[lax.rem(y + NY - k, NY)], y_send.at[k - 1], y_recv.at[k - 1], plane_at(2 * k)).wait_recv()
    final[core, z] = (got_y[0] + got_y[1] + got_y[2] + got_y[3]).astype(jnp.bfloat16)
    for k in range(1, NZ):
        copy = remote(final.at[core, z], final.at[core, z], g_send.at[k - 1], g_recv.at[k - 1], near_z[k - 1])
        copy.start()
        sent.append(copy)
    for k in range(NZ):
        there = lax.rem(z + NZ - k, NZ)
        if k > 0:
            remote(final.at[core, z], final.at[core, there], g_send.at[k - 1], g_recv.at[k - 1], near_z[k - 1]).wait_recv()
        copy = remote(final.at[core, there], final.at[core, there], d_send.at[k], d_recv.at[k], plane_at(1))
        copy.start()
        sent.append(copy)
    for k in range(NZ):
        there = lax.rem(z + NZ - k, NZ)
        remote(final.at[core, z], final.at[1 - core, there], d_send.at[k], d_recv.at[k], plane_at(1)).wait_recv()
    for copy in sent:
        copy.wait_send()


def finish_kernel(hid_ref, final_ref, out_ref, gs_ref, gn_ref):
    out_ref[...] = hid_ref[...]
    whole = final_ref[...].astype(jnp.float32).reshape(384, 256)
    gs_ref[...] = whole[:192]
    gn_ref[0:128] = whole[256:]
    gn_ref[128:192] = whole[192:256]


def on_device(features, owner_of, row_of, w_self, w_neighbor, cotangent):
    vmem = pl.BlockSpec(memory_space=pltpu.VMEM)
    dma = pltpu.SemaphoreType.DMA
    f32, bf16, i32 = jnp.float32, jnp.bfloat16, jnp.int32
    hidden, final = pl.pallas_call(
        step_kernel,
        out_shape=(jax.ShapeDtypeStruct((128, 256), bf16), jax.ShapeDtypeStruct((2, NZ, 24, 256), bf16)),
        in_specs=[pl.BlockSpec(memory_space=pl.ANY)] + [vmem] * 5,
        out_specs=(vmem, vmem),
        scratch_shapes=[
            pltpu.VMEM((192, 8192), bf16),
            pltpu.VMEM((256, 8192), bf16),
            pltpu.VMEM((192, 8192), bf16),
            pltpu.VMEM((8, 8, 256), i32),
            pltpu.VMEM((8, 8, 256), i32),
            pltpu.VMEM((8, 8, 256), i32),
            pltpu.VMEM((8, 8, 256), i32),
            pltpu.VMEM((8, 8, 256), i32),
            pltpu.SMEM((64, 256), i32),
            pltpu.VMEM((8, 1536), i32),
            pltpu.VMEM((16384, 128), f32),
            pltpu.VMEM((384, 128), f32),
            pltpu.VMEM((8, 8, 288, 128), bf16),
            pltpu.VMEM((8, 8, 288, 128), bf16),
            pltpu.VMEM((1024, 1536), bf16),
            pltpu.VMEM((1536, 256), bf16),
            pltpu.VMEM((1024, 256), f32),
            pltpu.VMEM((7, 3, 512, 128), bf16),
            pltpu.VMEM((7, 3, 512, 128), bf16),
            pltpu.VMEM((512, 384), bf16),
            pltpu.VMEM((384, 512), bf16),
            pltpu.VMEM((2, 64, 256), f32),
            pltpu.VMEM((NX - 1, 2, 64, 256), bf16),
            pltpu.VMEM((NX - 1, 2, 64, 256), bf16),
            pltpu.VMEM((NX, 2, 64, 256), bf16),
            pltpu.VMEM((2, NZ, 24, 256), f32),
            pltpu.VMEM((NZ, 24, 256), f32),
            pltpu.VMEM((NZ, 24, 256), f32),
            pltpu.VMEM((NZ, 24, 256), bf16),
            pltpu.VMEM((NZ - 1, 24, 256), bf16),
            pltpu.VMEM((NY, 24, 256), f32),
            dma(()), dma((NZ - 1,)), dma((NZ - 1,)), dma((8,)), dma((8,)), dma((8,)),
            dma((8, 8)), dma((8, 8)), dma((8,)), dma((7,)), dma((7,)),
            dma((NX - 1, 2)), dma((NX - 1, 2)), dma((NX - 1, 2)), dma((NX - 1, 2)), dma(()), dma(()),
            dma((NZ - 1,)), dma((NZ - 1,)), dma((NY - 1,)), dma((NY - 1,)),
            dma((NZ - 1,)), dma((NZ - 1,)), dma((NZ,)), dma((NZ,)),
        ],
        compiler_params=pltpu.CompilerParams(
            collective_id=1, has_side_effects=True, vmem_limit_bytes=60 * 1024 * 1024
        ),
        name="step",
    )(features, jnp.transpose(owner_of, (1, 2, 0)), jnp.transpose(row_of), w_self, w_neighbor, cotangent)
    return pl.pallas_call(
        finish_kernel,
        out_shape=(
            jax.ShapeDtypeStruct((128, 256), bf16),
            jax.ShapeDtypeStruct((192, 256), f32),
            jax.ShapeDtypeStruct((192, 256), f32),
        ),
        in_specs=[vmem, vmem],
        out_specs=(vmem, vmem, vmem),
        name="finish",
    )(hidden, final)


def solution(mesh):
    return jax.shard_map(
        on_device,
        mesh=mesh,
        in_specs=(
            P("narrow", "wide"),
            P("wide", None, None),
            P("wide", None),
            P("narrow", None),
            P("narrow", None),
            P(("wide", "narrow"), None),
        ),
        out_specs=(P(("wide", "narrow"), None), P("narrow", None), P("narrow", None)),
        check_vma=False,
    )
```
